512 devices in a mesh: ctx: 16 (over x, z_hi), row: 8 (over y), batch: 4 (over z_lo, core).
Axes of the slice: x: 4, y: 8, z: 8 (z_hi: 4, z_lo: 2; z = z_hi * 2 + z_lo), core: 2. Of those that a mesh axis runs over, the one named last changes fastest.
Arguments:
- queries: bfloat16 [12288, 5120], P(('batch', 'ctx'), 'row'), parts along dimension 0
- keys: bfloat16 [12288, 5120], P(('batch', 'ctx'), 'row'), parts along dimension 0
- values: bfloat16 [12288, 5120], P(('batch', 'ctx'), 'row'), parts along dimension 0, may hold values from -6 to 6
- gain_q: float32 [5120], P('row'), may hold values from 1.2 to 2.4
- gain_k: float32 [5120], P('row'), may hold values from 1.2 to 2.4
- clip_ids: int32 [12288], P(('batch', 'ctx')), parts along dimension 0, may hold values from 0 to 3, never falling along the last dimension, each value on 1 to 1920 neighbouring positions
- clip_grid: int32 [16, 2], P('batch'), parts along dimension 0, may hold values from 8 to 40
Outputs:
- attended: bfloat16 [12288, 5120], P(('batch', 'ctx'), 'row'), parts along dimension 0
The draws below stay inside these ranges and needn't reach their ends.
There are 4 independent parts, one for each index of `batch`. The reference program is written for one: setup_inputs(seed, part) draws one part's arguments, and reference() takes and returns one part's arrays. A program takes and returns all parts, laid end to end along the dimension named above; an argument that names none is the same for every part. Nothing has to cross between parts.
Inputs may be any that keep to these rules, and one draw needn't show every extreme that they name: `clip_ids`: never falls along the tokens; each of the 4 clips has 1 to 1920 tokens, and one has exactly 1920.
All inputs are finite; a program needn't handle non-finite values.
Results may differ from the reference program's by a relative error of at most 0.012.
The reference program's roundings to bfloat16 on the way count: a program that leaves them out, or rounds other values in their place, can miss the bound.
Values may be sent and summed in bfloat16 or wider, within the bound.
A program may use at most 64 MiB of HBM per device.

```python
import math
import jax
import jax.numpy as jnp
import numpy as np
from jax import lax

HEADS = 40
HD = 128
D = 5120
TOKENS = 3072
CLIPS = 4
MOST = 1920


def shared_field(key, which):
    columns = jnp.arange(D, dtype=jnp.float32)
    primary = jax.random.normal(jax.random.fold_in(key, 10 + which), (TOKENS, D), jnp.float32)
    rising = jnp.sqrt(1.0 + 2.0 * columns / (D - 1))
    row_scale = 10.0 ** jax.random.uniform(jax.random.fold_in(key, 30 + which), (TOKENS, 1), jnp.float32)
    column_scale = 10.0 ** jax.random.uniform(jax.random.fold_in(key, 40 + which), (1, D), jnp.float32) * rising[None, :]
    matrix = 0.3 * primary * row_scale * column_scale
    return matrix


def draw_queries(key, part):
    return shared_field(key, 0).astype(jnp.bfloat16)


def draw_keys(key, part):
    return shared_field(key, 1).astype(jnp.bfloat16)


def touch_ends(drawn, rng, smallest, top_value):
    dims = drawn.shape
    index_at = [jax.random.randint(jax.random.fold_in(rng, axis), (), 0, dims[axis]) for axis in range(len(dims))]
    drawn = drawn.at[tuple(index_at)].set(smallest)
    longest = dims.index(max(dims))
    index_at[longest] = (index_at[longest] + 1) % dims[longest]
    return drawn.at[tuple(index_at)].set(top_value)


def level_of(own_key, extent, shards, smallest, high):
    def one(position, shards_of):
        steps = jax.random.uniform(jax.random.fold_in(jax.random.fold_in(own_key, 6), position), (shards_of,), jnp.float32, smallest / len(shards), high / len(shards))
        return jnp.repeat(jnp.exp(steps), extent[position] // shards_of).reshape((-1,) + (1,) * (len(extent) - position - 1))

    loudness = one(*shards[0])
    for cut in shards[1:]:
        loudness = loudness * one(*cut)
    return loudness


def profile(number_of, total, limit, slope):
    weights = [(1 << 20) // math.isqrt(grade ** slope) + 1 for grade in range(2, number_of + 1)]
    spare, given = total - limit - (number_of - 1), [1] * (number_of - 1)
    while spare > 0:
        free = [i for i in range(number_of - 1) if given[i] < limit]
        mass, left = sum([weights[i] for i in free]), spare
        for i in free:
            more = min(limit - given[i], max(1, left * weights[i] // mass), spare)
            given[i] = given[i] + more
            spare = spare - more
    return np.array([limit] + given)


def ragged_sizes(stream_key, count, total, most, lean):
    if count == 2:
        one = jax.random.randint(stream_key, (), max(1, total - most), min(most, total - 1) + 1)
        return jnp.stack([one, total - one])
    lengths = jnp.asarray(profile(count, total, most, lean), jnp.int32)
    couples = (count - 1) // 2
    donor, receiver = lengths[1:1 + 2 * couples:2], lengths[2:2 + 2 * couples:2]
    margin = jnp.minimum(donor - 1, most - receiver)
    moved = jax.random.randint(jax.random.fold_in(stream_key, 1), (couples,), 0, 1 << 20) % (margin + 1)
    lengths = lengths.at[1:1 + 2 * couples:2].set(donor - moved).at[2:2 + 2 * couples:2].set(receiver + moved)
    return lengths[jax.random.permutation(jax.random.fold_in(stream_key, 2), count)]


def gaussian(key, extent, scale, limit, split=(), kind=jnp.bfloat16):
    level = level_of(key, extent, split, -0.22, 0.18) if split else 1.0
    values = jax.random.normal(key, extent, jnp.float32) * scale * level
    return jnp.minimum(jnp.maximum(values, -limit), limit).astype(kind)


def setup_inputs(seed: int = 0, part: int = 0) -> dict:
    seeds = jax.random.split(jax.random.key(seed), 8)
    part_keys = jax.random.split(jax.random.fold_in(seeds[7], part), 8)
    queries = draw_queries(jax.random.fold_in(jax.random.fold_in(seeds[7], part), 71), part)
    keys = draw_keys(jax.random.fold_in(jax.random.fold_in(seeds[7], part), 71), part)
    values = gaussian(part_keys[2], (TOKENS, D), 1.0, 6.0, ((0, 16), (1, 8)))
    gain_q = jnp.clip(1.2 + 1.2 * jax.random.uniform(seeds[3], (D,), jnp.float32) ** level_of(seeds[3], (D,), ((0, 8),), -0.2, 0.2), 1.2, 2.4)
    gain_k = jnp.clip(1.2 + 1.2 * jax.random.uniform(seeds[4], (D,), jnp.float32) ** level_of(seeds[4], (D,), ((0, 8),), -0.2, 0.2), 1.2, 2.4)
    clip_ids = jnp.searchsorted(jnp.cumsum(ragged_sizes(part_keys[5], CLIPS, TOKENS, MOST, 2)), jnp.arange(TOKENS), side="right").astype(jnp.int32)
    clip_grid = touch_ends(jax.random.randint(part_keys[6], (CLIPS, 2), 8, 41), jax.random.fold_in(part_keys[6], 1), 8, 40).astype(jnp.int32)
    return dict(queries=queries, keys=keys, values=values, gain_q=gain_q, gain_k=gain_k, clip_ids=clip_ids, clip_grid=clip_grid)


EPSILON = 1e-06
NEGATIVE = -1e+30
ROTARY_BASE = 10000.0

def lookup(lookup_table, positions):
    labels = jnp.arange(lookup_table.shape[0], dtype=jnp.int32)
    return lax.optimization_barrier(jnp.sum(jnp.where(positions[:, None] == labels[None, :], lookup_table[None, :], 0), axis=1))

def spin(matrix, offsets, clip_of, clip_grid, head_size):
    row_count = matrix.shape[0]
    sixth_part = head_size // 6
    first_dims = head_size - 4 * sixth_part
    first_freqs = 1.0 / ROTARY_BASE ** (jnp.arange(0, first_dims, 2, dtype=jnp.float32) / first_dims)
    other_freqs = 1.0 / ROTARY_BASE ** (jnp.arange(0, 2 * sixth_part, 2, dtype=jnp.float32) / (2 * sixth_part))
    heights = lookup(clip_grid[:, 0], clip_of)
    widths = lookup(clip_grid[:, 1], clip_of)
    frame_pos = offsets // (heights * widths)
    line_pos = offsets // widths % heights
    column_pos = offsets % widths
    angles = jnp.concatenate([frame_pos.astype(jnp.float32)[:, None] * first_freqs[None, :], line_pos.astype(jnp.float32)[:, None] * other_freqs[None, :], column_pos.astype(jnp.float32)[:, None] * other_freqs[None, :]], axis=1)
    cosine = jnp.repeat(jnp.cos(angles), 2, axis=1)
    sine_table = jnp.repeat(jnp.sin(angles), 2, axis=1)
    feature = jnp.arange(head_size, dtype=jnp.int32)
    is_even = (feature % 2 == 0)[None, None, :]
    head_view = matrix.reshape(row_count, -1, head_size)
    partner = jnp.where(is_even, -jnp.roll(head_view, -1, axis=2), jnp.roll(head_view, 1, axis=2))
    turned = head_view * cosine[:, None, :] + partner * sine_table[:, None, :]
    return turned.reshape(row_count, -1)

def reference(queries, keys, values, gain_q, gain_k, clip_ids, clip_grid):
    query_wide = queries.astype(jnp.float32)
    key_wide = keys.astype(jnp.float32)
    query_scale = lax.rsqrt(lax.optimization_barrier(jnp.sum(query_wide * query_wide, axis=1)) / D + EPSILON)
    key_scale = lax.rsqrt(lax.optimization_barrier(jnp.sum(key_wide * key_wide, axis=1)) / D + EPSILON)
    labels = jnp.arange(CLIPS, dtype=jnp.int32)
    counts = lax.optimization_barrier(jnp.sum((clip_ids[:, None] == labels[None, :]).astype(jnp.int32), axis=0))
    starts = jnp.cumsum(counts) - counts
    offsets = jnp.arange(TOKENS, dtype=jnp.int32) - lookup(starts, clip_ids)
    query_rot = spin(query_wide * query_scale[:, None] * gain_q[None, :], offsets, clip_ids, clip_grid, HD).astype(jnp.bfloat16)
    key_rot = spin(key_wide * key_scale[:, None] * gain_k[None, :], offsets, clip_ids, clip_grid, HD).astype(jnp.bfloat16)
    query_heads = jnp.transpose(query_rot.reshape(TOKENS, HEADS, HD), (1, 0, 2))
    key_heads = jnp.transpose(key_rot.reshape(TOKENS, HEADS, HD), (1, 0, 2))
    value_heads = jnp.transpose(values.reshape(TOKENS, HEADS, HD), (1, 0, 2))
    same = clip_ids[:, None] == clip_ids[None, :]
    score_scale = 1.0 / math.sqrt(HD)

    def one_head(operands):
        query_one, key_one, value_one = operands
        scores = jnp.dot(query_one, key_one.T, preferred_element_type=jnp.float32) * score_scale
        masked = jnp.where(same, scores, NEGATIVE)
        peak = lax.optimization_barrier(jnp.max(masked, axis=1))
        weights = jnp.where(same, jnp.exp(masked - peak[:, None]), 0.0)
        total_sum = lax.optimization_barrier(jnp.sum(weights, axis=1))
        summed = jnp.dot(weights.astype(jnp.bfloat16), value_one, preferred_element_type=jnp.float32)
        return summed / total_sum[:, None]
    outputs = lax.map(one_head, (query_heads, key_heads, value_heads))
    return jnp.transpose(outputs, (1, 0, 2)).reshape(TOKENS, D).astype(jnp.bfloat16)
```

```python
import functools
import math

import jax
import jax.numpy as jnp
import numpy as np
from jax import lax
from jax.experimental import pallas as pl
from jax.experimental.pallas import tpu as pltpu
from jax.sharding import PartitionSpec as P

HD = 128
CLIPS = 4
EPSILON = 1e-06
NEGATIVE = -1e30
ROTARY_BASE = 10000.0
SIDE = 4
MESH = pl.DeviceIdType.MESH


def frequencies():
    p = HD // 6
    f = HD - 4 * p
    base = np.float32(ROTARY_BASE)
    first = np.float32(1.0) / base ** (np.arange(0, f, 2, dtype=np.float32) / np.float32(f))
    other = np.float32(1.0) / base ** (np.arange(0, 2 * p, 2, dtype=np.float32) / np.float32(2 * p))
    return np.repeat(np.concatenate([first, other, other]), 2)[None, :].astype(np.float32), f, f + 2 * p


def cols(h):
    if isinstance(h, int):
        return pl.ds(h * HD, HD)
    return pl.ds(pl.multiple_of(h * HD, HD), HD)


def kernel(
    rows_n, model, cut_a, cut_b,
    q, k, v, gq, gk, ids, freq, grid, out,
    pad, ssq_send, ssq_recv, cz_send, cz_recv, cx_send, cx_recv,
    krot, qrot, kh, vh, k4, v4, qh, q4, s_scr, o_send, o4_send, o4_recv, st_send, st_recv, starts_scr,
    sem_bs, sem_br, sem_zs, sem_zr, sem_xs, sem_xr, sem_os, sem_or,
):
    T = q.shape[0]
    me = lax.axis_index("ctx")
    row = lax.axis_index("row")
    x = me // SIDE
    z = lax.rem(me, SIDE)
    zs = [lax.rem(z + d, SIDE) for d in range(SIDE)]
    xs = [lax.rem(x + d, SIDE) for d in range(SIDE)]
    zpeer = [x * SIDE + a for a in zs]
    xpeer = [a * SIDE + z for a in xs]
    zsrc = [lax.rem(z + SIDE - d, SIDE) for d in range(SIDE)]
    xsrc = [lax.rem(x + SIDE - d, SIDE) for d in range(SIDE)]
    scale = 1.0 / math.sqrt(HD)

    barrier = pltpu.get_barrier_semaphore()
    for d in range(1, SIDE):
        pl.semaphore_signal(barrier, inc=1, device_id={"ctx": zpeer[d]}, device_id_type=MESH)
        pl.semaphore_signal(barrier, inc=1, device_id={"ctx": xpeer[d]}, device_id_type=MESH)
    for d in range(1, rows_n):
        pl.semaphore_signal(
            barrier, inc=1, device_id={"row": lax.rem(row + d, rows_n)}, device_id_type=MESH
        )

    sends = []

    def send(src, dst, ss, rs, where):
        c = pltpu.make_async_remote_copy(
            src_ref=src, dst_ref=dst, send_sem=ss, recv_sem=rs, device_id=where, device_id_type=MESH
        )
        c.start()
        sends.append(c)
        return c

    pad[T:, :] = jnp.zeros((pad.shape[0] - T, HD), jnp.float32)
    ssq_send[...] = jnp.zeros_like(ssq_send)
    for i, ref in enumerate((q, k)):
        acc = None
        for h in range(5):
            w = ref[:, h * HD : (h + 1) * HD].astype(jnp.float32)
            acc = w * w if acc is None else acc + w * w
        pad[:T, :] = acc
        ssq_send[i : i + 1, :] = jnp.sum(jnp.transpose(pad[...]), axis=0, keepdims=True)
    idrow = ids[...]
    level = lax.broadcasted_iota(jnp.int32, (8, T), 0)
    below = jnp.where(jnp.broadcast_to(idrow, (8, T)) < level, 1.0, 0.0).astype(jnp.float32)
    counts = jnp.broadcast_to(jnp.sum(below, axis=1, keepdims=True), (8, HD))
    cz_send[...] = counts

    pl.semaphore_wait(barrier, 2 * (SIDE - 1) + rows_n - 1)

    cz = [
        send(cz_send, cz_recv.at[d], sem_bs.at[d], sem_br.at[d], {"ctx": zpeer[d]})
        for d in range(1, SIDE)
    ]
    sq = [
        send(
            ssq_send, ssq_recv.at[d], sem_bs.at[8 + d], sem_br.at[8 + d],
            {"row": lax.rem(row + d, rows_n)},
        )
        for d in range(1, rows_n)
    ]

    def to_z(n, src, dst_own, dst_four):
        four = []
        own = []
        for d in (2, 1, 3):
            if dst_four is not None:
                four.append((d, send(
                    src.at[:, cols(4)], dst_four.at[z], sem_zs.at[n, 0, d], sem_zr.at[n, 0, d],
                    {"ctx": zpeer[d]},
                )))
        for d in (2, 1, 3):
            own.append((d, send(
                src.at[:, cols(zs[d])], dst_own, sem_zs.at[n, 1, d], sem_zr.at[n, 1, d],
                {"ctx": zpeer[d]},
            )))
        return dict(four), dict(own)

    def to_x(n, j, src, dst):
        return [
            send(src, dst, sem_xs.at[n, j, d], sem_xr.at[n, j, d], {"ctx": xpeer[d]})
            for d in (2, 1, 3)
        ]

    v_four, v_own = to_z(0, v, vh.at[me], v4)

    for c in cz:
        c.wait_recv()
    part = cz_send[...]
    for d in range(1, SIDE):
        part = part + cz_recv[d]
    cx_send[...] = part
    vx = [to_x(0, 0, v.at[:, cols(z)], vh.at[me])]
    vh[me] = v[:, cols(z)]
    v4[z] = v[:, cols(4)]
    cx = [
        send(cx_send, cx_recv.at[d], sem_bs.at[4 + d], sem_br.at[4 + d], {"ctx": xpeer[d]})
        for d in range(1, SIDE)
    ]
    for c in cx:
        c.wait_recv()
    starts = cx_send[...]
    for d in range(1, SIDE):
        starts = starts + cx_recv[d]
    starts_scr[...] = starts

    lane = lax.broadcasted_iota(jnp.int32, (T, HD), 1)
    token = (lax.broadcasted_iota(jnp.int32, (T, HD), 0) + me * T).astype(jnp.float32)
    first = jnp.zeros((T, HD), jnp.float32)
    height = jnp.full((T, HD), grid[0, 0].astype(jnp.float32))
    width = jnp.full((T, HD), grid[0, 1].astype(jnp.float32))
    for c in range(1, CLIPS):
        s = jnp.broadcast_to(starts[c : c + 1, :], (T, HD))
        inside = token >= s
        first = jnp.where(inside, s, first)
        height = jnp.where(inside, grid[c, 0].astype(jnp.float32), height)
        width = jnp.where(inside, grid[c, 1].astype(jnp.float32), width)
    offset = token - first
    frame = jnp.floor((offset + 0.5) / (height * width))
    lines = jnp.floor((offset + 0.5) / width)
    line = lines - height * jnp.floor((lines + 0.5) / height)
    column = offset - width * lines
    place = jnp.where(lane < cut_a, frame, jnp.where(lane < cut_b, line, column))
    angle = place * freq[...]
    cosine = jnp.cos(angle)
    even = lax.rem(lane, 2) == 0
    sine = jnp.sin(angle)

    for c in sq:
        c.wait_recv()
    total = ssq_send[...]
    for d in range(1, rows_n):
        total = total + ssq_recv[d]
    rs = lax.rsqrt(total / model + EPSILON)

    def rope(src, dst, gain, i):
        col = jnp.transpose(jnp.broadcast_to(rs[i : i + 1, :], (HD, rs.shape[1])))[:T, :]
        for h in (4, 0, 1, 2, 3):
            a = src[:, h * HD : (h + 1) * HD].astype(jnp.float32) * col
            a = a * gain[:, h * HD : (h + 1) * HD]
            partner = jnp.where(even, -pltpu.roll(a, HD - 1, 1), pltpu.roll(a, 1, 1))
            dst[:, h * HD : (h + 1) * HD] = (a * cosine + partner * sine).astype(jnp.bfloat16)

    rope(k, krot, gk, 1)
    kh[me] = krot[:, cols(z)]
    k4[z] = krot[:, cols(4)]
    k_four, k_own = to_z(1, krot, kh.at[me], k4)
    kx = [to_x(1, 0, krot.at[:, cols(z)], kh.at[me])]
    rope(q, qrot, gq, 0)
    qh[z] = qrot[:, cols(z)]
    q4[x] = qrot[:, cols(4)]
    q4s = [
        send(qrot.at[:, cols(4)], q4.at[x], sem_xs.at[2, 0, d], sem_xr.at[2, 0, d], {"ctx": xpeer[d]})
        for d in (2, 1, 3)
    ]
    _, q_own = to_z(2, qrot, qh.at[z], None)

    for j in (1, 3, 2):
        v_own[j].wait_recv()
        slot = vh.at[x * SIDE + zsrc[j]]
        vx.append(to_x(0, j, slot, slot))

    def clip_cols(first_token):
        t = (lax.broadcasted_iota(jnp.int32, (T, HD), 0) + first_token).astype(jnp.float32)
        c = jnp.zeros((T, HD), jnp.float32)
        for i in range(1, CLIPS):
            c = c + jnp.where(t >= starts_scr[i : i + 1, :], 1.0, 0.0)
        return c

    def clip_row(first_token):
        t = (lax.broadcasted_iota(jnp.int32, (1, wide), 1) + first_token).astype(jnp.float32)
        c = jnp.zeros((1, wide), jnp.float32)
        for i in range(1, CLIPS):
            edge = jnp.max(starts_scr[i : i + 1, :], axis=1, keepdims=True)
            c = c + jnp.where(t >= edge, 1.0, 0.0)
        return c

    wide = SIDE * T

    def attend(query, q_first, kref, vref, blocks, firsts):
        qc = clip_cols(q_first)[:, :1]
        peak = None
        for b in range(blocks):
            s = lax.dot_general(
                query, kref[SIDE * b : SIDE * b + SIDE].reshape(wide, HD), (((1,), (1,)), ((), ())),
                preferred_element_type=jnp.float32,
            )
            s = jnp.where(qc == clip_row(firsts(b)), s, NEGATIVE)
            s_scr[b] = s
            m = jnp.max(s, axis=1, keepdims=True)
            peak = m if peak is None else jnp.maximum(peak, m)
        summed = jnp.zeros((T, HD), jnp.float32)
        weight = jnp.zeros((T, 1), jnp.float32)
        for b in range(blocks):
            w = jnp.exp((s_scr[b] - peak) * scale)
            weight = weight + jnp.sum(w, axis=1, keepdims=True)
            summed = summed + jnp.dot(
                w.astype(jnp.bfloat16), vref[SIDE * b : SIDE * b + SIDE].reshape(wide, HD),
                preferred_element_type=jnp.float32,
            )
        return summed, weight, peak * scale

    for d in (1, 3, 2):
        v_four[d].wait_recv()
        k_four[d].wait_recv()
    for c in q4s:
        c.wait_recv()

    def four_body(i, carry):
        o, w, m = attend(q4[i], (i * SIDE + z) * T, k4, v4, 1, lambda b: x * wide)
        o4_send[i] = (o / w).astype(jnp.bfloat16)
        lanes = lax.broadcasted_iota(jnp.int32, (T, HD), 1)
        pad[:T, :] = jnp.where(lanes == 0, m, jnp.where(lanes == 1, w, 0.0))
        st_send[i] = jnp.transpose(pad[...])[:8, :]
        return carry

    lax.fori_loop(0, SIDE, four_body, 0)
    o4s = []
    for d in (2, 1, 3):
        o4s.append(send(
            o4_send.at[xs[d]], o4_recv.at[x], sem_os.at[0, d], sem_or.at[0, d], {"ctx": xpeer[d]}
        ))
        o4s.append(send(
            st_send.at[xs[d]], st_recv.at[x], sem_os.at[1, d], sem_or.at[1, d], {"ctx": xpeer[d]}
        ))

    for j in (1, 3, 2):
        k_own[j].wait_recv()
        slot = kh.at[x * SIDE + zsrc[j]]
        kx.append(to_x(1, j, slot, slot))
    for group in vx + kx:
        for c in group:
            c.wait_recv()

    backs = []
    for n in (2, 1, 3, 0):
        a = zs[n]
        if n:
            q_own[SIDE - n].wait_recv()
        o, w, _ = attend(qh[a], (x * SIDE + a) * T, kh, vh, SIDE, lambda b: b * wide)
        o = (o / w).astype(jnp.bfloat16)
        if n:
            o_send[n] = o
            backs.append(send(
                o_send.at[n], out.at[:, cols(z)], sem_os.at[2, n], sem_or.at[2, n], {"ctx": zpeer[n]}
            ))
        else:
            out[:, cols(z)] = o

    for c in o4s:
        c.wait_recv()
    o4_recv[x] = o4_send[x]
    st_recv[x] = st_send[x]
    means, totals, peaks = [], [], []
    for i in range(SIDE):
        pad128 = jnp.concatenate(
            [st_recv[i], jnp.zeros((HD - 8, st_recv.shape[2]), jnp.float32)], axis=0
        )
        st = jnp.transpose(pad128)[:T, :]
        peaks.append(st[:, 0:1])
        totals.append(st[:, 1:2])
    peak = functools.reduce(jnp.maximum, peaks)
    num = jnp.zeros((T, HD), jnp.float32)
    den = jnp.zeros((T, 1), jnp.float32)
    for i in range(SIDE):
        f = totals[i] * jnp.exp(peaks[i] - peak)
        den = den + f
        num = num + f * o4_recv[i].astype(jnp.float32)
    out[:, cols(4)] = (num / den).astype(jnp.bfloat16)

    for c in backs:
        c.wait_recv()
    for c in sends:
        c.wait_send()


def on_device(rows_n, queries, keys, values, gain_q, gain_k, clip_ids, clip_grid):
    T, width = queries.shape
    freq, cut_a, cut_b = frequencies()
    bf, f32 = jnp.bfloat16, jnp.float32
    vm = pl.BlockSpec(memory_space=pltpu.VMEM)
    dma = pltpu.SemaphoreType.DMA
    block = (T, HD)
    return pl.pallas_call(
        functools.partial(kernel, rows_n, float(width * rows_n), cut_a, cut_b),
        out_shape=jax.ShapeDtypeStruct((T, width), bf),
        in_specs=[vm] * 7 + [pl.BlockSpec(memory_space=pltpu.SMEM)],
        out_specs=vm,
        scratch_shapes=[
            pltpu.VMEM((256, HD), f32),
            pltpu.VMEM((8, 256), f32),
            pltpu.VMEM((rows_n, 8, 256), f32),
            pltpu.VMEM((8, HD), f32),
            pltpu.VMEM((SIDE, 8, HD), f32),
            pltpu.VMEM((8, HD), f32),
            pltpu.VMEM((SIDE, 8, HD), f32),
            pltpu.VMEM((T, width), bf),
            pltpu.VMEM((T, width), bf),
            pltpu.VMEM((SIDE * SIDE,) + block, bf),
            pltpu.VMEM((SIDE * SIDE,) + block, bf),
            pltpu.VMEM((SIDE,) + block, bf),
            pltpu.VMEM((SIDE,) + block, bf),
            pltpu.VMEM((SIDE,) + block, bf),
            pltpu.VMEM((SIDE,) + block, bf),
            pltpu.VMEM((SIDE, T, SIDE * T), f32),
            pltpu.VMEM((SIDE,) + block, bf),
            pltpu.VMEM((SIDE,) + block, bf),
            pltpu.VMEM((SIDE,) + block, bf),
            pltpu.VMEM((SIDE, 8, 256), f32),
            pltpu.VMEM((SIDE, 8, 256), f32),
            pltpu.VMEM((8, HD), f32),
            dma((16,)),
            dma((16,)),
            dma((3, 2, SIDE)),
            dma((3, 2, SIDE)),
            dma((3, SIDE, SIDE)),
            dma((3, SIDE, SIDE)),
            dma((3, SIDE)),
            dma((3, SIDE)),
        ],
        compiler_params=pltpu.CompilerParams(
            collective_id=0, has_side_effects=True, vmem_limit_bytes=48 * 1024 * 1024
        ),
        name="clip_attention",
    )(
        queries, keys, values, gain_q[None, :], gain_k[None, :], clip_ids[None, :],
        jnp.asarray(freq), clip_grid,
    )


def solution(mesh):
    in_specs = (
        P(("batch", "ctx"), "row"),
        P(("batch", "ctx"), "row"),
        P(("batch", "ctx"), "row"),
        P("row"),
        P("row"),
        P(("batch", "ctx")),
        P("batch", None),
    )
    out_specs = P(("batch", "ctx"), "row")
    return jax.shard_map(
        functools.partial(on_device, mesh.shape["row"]),
        mesh=mesh, in_specs=in_specs, out_specs=out_specs, check_vma=False,
    )
```

```python
import functools
import math

import jax
import jax.numpy as jnp
import numpy as np
from jax import lax
from jax.experimental import pallas as pl
from jax.experimental.pallas import tpu as pltpu
from jax.sharding import PartitionSpec as P

HD = 128
CLIPS = 4
EPSILON = 1e-06
NEGATIVE = -1e30
ROTARY_BASE = 10000.0
LOG2E = math.log2(math.e)
SIDE = 4
MESH = pl.DeviceIdType.MESH


def frequencies():
    p = HD // 6
    f = HD - 4 * p
    base = np.float32(ROTARY_BASE)
    first = np.float32(1.0) / base ** (np.arange(0, f, 2, dtype=np.float32) / np.float32(f))
    other = np.float32(1.0) / base ** (np.arange(0, 2 * p, 2, dtype=np.float32) / np.float32(2 * p))
    return np.repeat(np.concatenate([first, other, other]), 2)[None, :].astype(np.float32), f, f + 2 * p


def cols(h):
    if isinstance(h, int):
        return pl.ds(h * HD, HD)
    return pl.ds(pl.multiple_of(h * HD, HD), HD)


def kernel(
    rows_n, model, cut_a, cut_b,
    q_hbm, k_hbm, v, gq_hbm, gk_hbm, ids_hbm, freq_hbm, grid_hbm, out,
    q, k, gq, gk, ids, freq, grid, pad, ssq_send, ssq_recv, cz_send, cz_recv, cx_send, cx_recv,
    krot, qrot, kh, vh, k4, v4, qh, q4, m_scr, s_scr, a_scr, o_send, o4_send, o4_recv, st_send, st_recv, starts_scr,
    sem_s, sem_r, sem_zr, sem_xr, sem_in,
):
    T = q.shape[0]
    me = lax.axis_index("ctx")
    row = lax.axis_index("row")
    x = me // SIDE
    z = lax.rem(me, SIDE)
    zs = [lax.rem(z + d, SIDE) for d in range(SIDE)]
    xs = [lax.rem(x + d, SIDE) for d in range(SIDE)]
    zpeer = [x * SIDE + a for a in zs]
    xpeer = [a * SIDE + z for a in xs]
    zsrc = [lax.rem(z + SIDE - d, SIDE) for d in range(SIDE)]
    xsrc = [lax.rem(x + SIDE - d, SIDE) for d in range(SIDE)]
    scale = 1.0 / math.sqrt(HD)
    wide = SIDE * T

    def left(ref, i):
        return ref.at[i, :, 0:HD]

    barrier = pltpu.get_barrier_semaphore()
    for d in range(1, SIDE):
        pl.semaphore_signal(barrier, inc=1, device_id={"ctx": zpeer[d]}, device_id_type=MESH)
        pl.semaphore_signal(barrier, inc=1, device_id={"ctx": xpeer[d]}, device_id_type=MESH)
    for d in range(1, rows_n):
        pl.semaphore_signal(
            barrier, inc=1, device_id={"row": lax.rem(row + d, rows_n)}, device_id_type=MESH
        )
    loads = [
        pltpu.make_async_copy(src, dst, sem_in.at[i])
        for i, (src, dst) in enumerate([
            (ids_hbm, ids), (q_hbm, q), (k_hbm, k), (grid_hbm, grid), (freq_hbm, freq),
            (gk_hbm, gk), (gq_hbm, gq), (v.at[:, cols(z)], left(vh, z)), (v.at[:, cols(4)], left(v4, z)),
        ])
    ]
    for c in loads:
        c.start()

    def send(src, dst, group, arrival, where):
        pltpu.make_async_remote_copy(
            src_ref=src, dst_ref=dst, send_sem=sem_s.at[group], recv_sem=arrival, device_id=where,
            device_id_type=MESH,
        ).start()

    def done(ref, sem):
        pltpu.make_async_copy(ref, ref, sem).wait()

    def to_z(n, src, dst):
        for d in (1, 3, 2):
            send(src.at[:, cols(zs[d])], dst, 2 + n, sem_zr.at[n, d], {"ctx": zpeer[d]})

    def four_to_z(n, src, dst):
        for d in (1, 3, 2):
            send(src.at[:, cols(4)], left(dst, z), 2 + n, sem_r.at[n], {"ctx": zpeer[d]})

    def to_x(n, src, dst, a):
        for d in (1, 3, 2):
            send(src, left(dst, d * SIDE + a), n, sem_xr.at[n], {"ctx": xpeer[d]})

    loads[0].wait()
    level = lax.broadcasted_iota(jnp.int32, (8, T), 0)
    below = jnp.where(jnp.broadcast_to(ids[...], (8, T)) < level, 1.0, 0.0).astype(jnp.float32)
    cz_send[...] = jnp.broadcast_to(jnp.sum(below, axis=1, keepdims=True), (8, HD))

    with jax.named_scope("entry_wait"):
        pl.semaphore_wait(barrier, 2 * (SIDE - 1) + rows_n - 1)

    for d in range(1, SIDE):
        send(cz_send, cz_recv.at[d], 6, sem_r.at[3], {"ctx": zpeer[d]})
    to_z(0, v, left(vh, z))
    to_x(0, v.at[:, cols(z)], vh, z)
    four_to_z(0, v, v4)

    with jax.named_scope("squares"):
        pad[T:256, :] = jnp.zeros((256 - T, HD), jnp.float32)
        ssq_send[...] = jnp.zeros_like(ssq_send)
        for i, ref in enumerate((q, k)):
            loads[1 + i].wait()
            acc = None
            for h in range(5):
                w = ref[:, h * HD : (h + 1) * HD].astype(jnp.float32)
                acc = w * w if acc is None else acc + w * w
            pad[:T, :] = acc
            ssq_send[i : i + 1, :] = jnp.sum(jnp.transpose(pad[0:256, :]), axis=0, keepdims=True)
    for d in range(1, rows_n):
        send(
            ssq_send, ssq_recv.at[d], 7, sem_r.at[5], {"row": lax.rem(row + d, rows_n)}
        )

    with jax.named_scope("count_z_wait"):
        done(cz_recv.at[1:SIDE], sem_r.at[3])
    part = cz_send[...]
    for d in range(1, SIDE):
        part = part + cz_recv[d]
    cx_send[...] = part
    for d in range(1, SIDE):
        send(cx_send, cx_recv.at[d], 6, sem_r.at[4], {"ctx": xpeer[d]})

    def forward(n, ref, j):
        slot = left(ref, zsrc[j])
        with jax.named_scope("%s_wait%d" % ("vk"[n], j)):
            done(slot, sem_zr.at[n, j])
        to_x(n, slot, ref, zsrc[j])

    forward(0, vh, 1)
    forward(0, vh, 3)
    with jax.named_scope("count_x_wait"):
        done(cx_recv.at[1:SIDE], sem_r.at[4])
    starts = cx_send[...]
    for d in range(1, SIDE):
        starts = starts + cx_recv[d]
    starts_scr[...] = starts

    for c in loads[3:]:
        c.wait()
    lane = lax.broadcasted_iota(jnp.int32, (T, HD), 1)
    token = (lax.broadcasted_iota(jnp.int32, (T, HD), 0) + me * T).astype(jnp.float32)
    first = jnp.zeros((T, HD), jnp.float32)
    shape_of = grid[...].astype(jnp.float32)
    height = jnp.broadcast_to(shape_of[0:1, 0:1], (T, HD))
    width = jnp.broadcast_to(shape_of[1:2, 0:1], (T, HD))
    for c in range(1, CLIPS):
        s = jnp.broadcast_to(starts[c : c + 1, :], (T, HD))
        inside = token >= s
        first = jnp.where(inside, s, first)
        height = jnp.where(inside, shape_of[0:1, c : c + 1], height)
        width = jnp.where(inside, shape_of[1:2, c : c + 1], width)
    offset = token - first
    frame = jnp.floor((offset + 0.5) / (height * width))
    lines = jnp.floor((offset + 0.5) / width)
    line = lines - height * jnp.floor((lines + 0.5) / height)
    column = offset - width * lines
    place = jnp.where(lane < cut_a, frame, jnp.where(lane < cut_b, line, column))
    angle = place * freq[...]
    with jax.named_scope("trig"):
        cosine = jnp.cos(angle)
    even = lax.rem(lane, 2) == 0
    sine = jnp.sin(angle)

    with jax.named_scope("square_wait"):
        if rows_n > 1:
            done(ssq_recv.at[1:rows_n], sem_r.at[5])
    total = ssq_send[...]
    for d in range(1, rows_n):
        total = total + ssq_recv[d]
    rs = lax.rsqrt(total / model + EPSILON)

    def rope(src, dst, gain, i):
        col = jnp.transpose(jnp.broadcast_to(rs[i : i + 1, :], (HD, rs.shape[1])))[:T, :]
        for h in (4, 0, 1, 2, 3):
            a = src[:, h * HD : (h + 1) * HD].astype(jnp.float32) * col
            a = a * gain[h * HD : (h + 1) * HD].reshape(1, HD)
            partner = jnp.where(even, -pltpu.roll(a, HD - 1, 1), pltpu.roll(a, 1, 1))
            dst[:, h * HD : (h + 1) * HD] = (a * cosine + partner * sine).astype(jnp.bfloat16)

    with jax.named_scope("rope_k"):
        rope(k, krot, gk, 1)
    to_z(1, krot, left(kh, z))
    to_x(1, krot.at[:, cols(z)], kh, z)
    forward(0, vh, 2)
    with jax.named_scope("rope_q"):
        rope(q, qrot, gq, 0)
    for d in (1, 3, 2):
        send(qrot.at[:, cols(zs[d])], left(qh, z), 4, sem_zr.at[2, d], {"ctx": zpeer[d]})
    four_to_z(1, krot, k4)
    kh[z, :, 0:HD] = krot[:, cols(z)]
    k4[z, :, 0:HD] = krot[:, cols(4)]
    qh[z, :, 0:HD] = qrot[:, cols(z)]
    q4[x, :, 0:HD] = qrot[:, cols(4)]

    lanes = lax.broadcasted_iota(jnp.int32, (T, HD), 1)

    def member(first_token, inside, outside):
        t = (lax.broadcasted_iota(jnp.int32, (T, HD), 0) + first_token).astype(jnp.float32)
        c = jnp.zeros((T, HD), jnp.int32)
        for i in range(1, CLIPS):
            c = c + jnp.where(t >= starts_scr[i : i + 1, :], 1, 0)
        value = jnp.where(c == lanes, inside, outside)
        return jnp.where(lanes < CLIPS, value, 0.0).astype(jnp.bfloat16)

    ones = jnp.ones((T, HD), jnp.bfloat16)

    def fill(i, carry):
        vh[i, :, HD:] = ones
        block = lax.rem(x + SIDE - i // SIDE, SIDE) * SIDE + lax.rem(i, SIDE)
        kh[i, :, HD:] = member(block * T, 1.0, 0.0)
        return carry

    def fill_four(i, carry):
        v4[i, :, HD:] = ones
        k4[i, :, HD:] = member((x * SIDE + i) * T, 1.0, 0.0)
        qh[i, :, HD:] = member((x * SIDE + i) * T, 0.0, NEGATIVE)
        q4[i, :, HD:] = member((i * SIDE + z) * T, 0.0, NEGATIVE)
        return carry

    with jax.named_scope("fill"):
        lax.fori_loop(0, SIDE, fill_four, 0)
        lax.fori_loop(0, SIDE * SIDE, fill, 0)
    for j in (1, 3, 2):
        forward(1, kh, j)
    for d in (1, 3, 2):
        send(qrot.at[:, cols(4)], left(q4, x), 4, sem_r.at[2], {"ctx": xpeer[d]})

    third = wide // 3

    def attend(queries, keys, vals, carried=None):
        keys = keys.reshape(-1, 2 * HD)
        vals = vals.reshape(-1, 2 * HD)
        n = keys.shape[0]
        for t in range(3):
            tile = pl.ds(t * third, third)
            s = lax.dot_general(
                queries[t * third : (t + 1) * third], keys, (((1,), (1,)), ((), ())),
                preferred_element_type=jnp.float32,
            )
            s_scr[t, :, 0:n] = s
            m = jnp.max(s, axis=1, keepdims=True)
            if carried:
                old = m_scr[tile, 0:1]
                m = jnp.maximum(m, old)
                factor = jnp.exp2((old - m) * (scale * LOG2E))
            w = jnp.exp2((s_scr[t, :, 0:n] - m) * (scale * LOG2E)).astype(jnp.bfloat16)
            o = jnp.dot(w, vals, preferred_element_type=jnp.float32)
            if carried:
                o = o + a_scr[tile, :] * factor
            a_scr[tile, :] = o
            m_scr[tile, :] = jnp.broadcast_to(m, (third, HD))

    def divide(o):
        return (o[:, :HD] / o[:, HD:]).astype(jnp.bfloat16)

    with jax.named_scope("q_wait"):
        for n in (3, 1, 2):
            done(left(qh, zs[n]), sem_zr.at[2, SIDE - n])
    with jax.named_scope("own_attend"):
        attend(qh[...].reshape(wide, 2 * HD), kh[0:SIDE], vh[0:SIDE])
    with jax.named_scope("x_wait"):
        done(left(vh, pl.ds(SIDE, 3 * SIDE)), sem_xr.at[0])
        done(left(kh, pl.ds(SIDE, 3 * SIDE)), sem_xr.at[1])
    with jax.named_scope("x_attend"):
        attend(qh[...].reshape(wide, 2 * HD), kh[SIDE:], vh[SIDE:], True)
        o_send[...] = divide(a_scr[...]).reshape(SIDE, T, HD)
    for n in (2, 1, 3):
        send(o_send.at[zs[n]], out.at[:, cols(z)], 5, sem_r.at[6], {"ctx": zpeer[n]})
    out[:, cols(z)] = o_send[z]

    with jax.named_scope("four_wait"):
        done(left(v4, pl.ds(0, SIDE - 1)), sem_r.at[0])
        done(left(k4, pl.ds(0, SIDE - 1)), sem_r.at[1])
        done(left(q4, pl.ds(0, SIDE - 1)), sem_r.at[2])
    with jax.named_scope("four_attend"):
        pad[wide:, :] = jnp.zeros((64, HD), jnp.float32)
        attend(q4[...].reshape(wide, 2 * HD), k4[...], v4[...])
        m, o = m_scr[...], a_scr[...]
        o4_send[...] = divide(o).reshape(SIDE, T, HD)
        flags = lax.broadcasted_iota(jnp.int32, (wide, HD), 1)
        pad[0:wide, :] = jnp.where(flags == 0, m * scale, jnp.where(flags == 1, o[:, HD:], 0.0))
        for i in range(SIDE):
            st_send[i] = jnp.transpose(pad[i * T : i * T + 256, :])[:8, :]
    for d in (1, 3, 2):
        send(o4_send.at[xs[d]], o4_recv.at[x], 5, sem_r.at[7], {"ctx": xpeer[d]})
        send(st_send.at[xs[d]], st_recv.at[x], 8, sem_r.at[8], {"ctx": xpeer[d]})
    o4_recv[x] = o4_send[x]
    st_recv[x] = st_send[x]
    with jax.named_scope("four_back_wait"):
        done(o4_recv.at[0 : SIDE - 1], sem_r.at[7])
        done(st_recv.at[0 : SIDE - 1], sem_r.at[8])
    totals, peaks = [], []
    for i in range(SIDE):
        pad128 = jnp.concatenate(
            [st_recv[i], jnp.zeros((HD - 8, st_recv.shape[2]), jnp.float32)], axis=0
        )
        st = jnp.transpose(pad128)[:T, :]
        peaks.append(st[:, 0:1])
        totals.append(st[:, 1:2])
    peak = functools.reduce(jnp.maximum, peaks)
    num = jnp.zeros((T, HD), jnp.float32)
    den = jnp.zeros((T, 1), jnp.float32)
    for i in range(SIDE):
        f = totals[i] * jnp.exp(peaks[i] - peak)
        den = den + f
        num = num + f * o4_recv[i].astype(jnp.float32)
    out[:, cols(4)] = (num / den).astype(jnp.bfloat16)

    with jax.named_scope("back_wait"):
        done(o4_recv.at[0 : SIDE - 1], sem_r.at[6])
    with jax.named_scope("send_wait"):
        done(left(vh, pl.ds(0, 3 * SIDE)), sem_s.at[0])
        done(left(kh, pl.ds(0, 3 * SIDE)), sem_s.at[1])
        for group in range(2, 6):
            done(left(vh, pl.ds(0, 6)), sem_s.at[group])
        done(st_recv.at[0 : SIDE - 1], sem_s.at[6])
        if rows_n > 1:
            done(ssq_recv.at[1:rows_n], sem_s.at[7])
        done(st_recv.at[0 : SIDE - 1], sem_s.at[8])


def on_device(rows_n, queries, keys, values, gain_q, gain_k, clip_ids, clip_grid):
    T, width = queries.shape
    freq, cut_a, cut_b = frequencies()
    bf, f32 = jnp.bfloat16, jnp.float32
    vm = pl.BlockSpec(memory_space=pltpu.VMEM)
    dma = pltpu.SemaphoreType.DMA
    block = (T, HD)
    return pl.pallas_call(
        functools.partial(kernel, rows_n, float(width * rows_n), cut_a, cut_b),
        out_shape=pltpu.VMEM((T, width), bf),
        in_specs=[pl.BlockSpec(memory_space=pltpu.HBM)] * 8,
        out_specs=vm,
        scratch_shapes=[
            pltpu.VMEM((T, width), bf),
            pltpu.VMEM((T, width), bf),
            pltpu.VMEM((width,), f32),
            pltpu.VMEM((width,), f32),
            pltpu.VMEM((1, T), jnp.int32),
            pltpu.VMEM((1, HD), f32),
            pltpu.VMEM((2, CLIPS), jnp.int32),
            pltpu.VMEM((SIDE * T + 64, HD), f32),
            pltpu.VMEM((8, 256), f32),
            pltpu.VMEM((rows_n, 8, 256), f32),
            pltpu.VMEM((8, HD), f32),
            pltpu.VMEM((SIDE, 8, HD), f32),
            pltpu.VMEM((8, HD), f32),
            pltpu.VMEM((SIDE, 8, HD), f32),
            pltpu.VMEM((T, width), bf),
            pltpu.VMEM((T, width), bf),
            pltpu.VMEM((SIDE * SIDE, T, 2 * HD), bf),
            pltpu.VMEM((SIDE * SIDE, T, 2 * HD), bf),
            pltpu.VMEM((SIDE, T, 2 * HD), bf),
            pltpu.VMEM((SIDE, T, 2 * HD), bf),
            pltpu.VMEM((SIDE, T, 2 * HD), bf),
            pltpu.VMEM((SIDE, T, 2 * HD), bf),
            pltpu.VMEM((SIDE * T, HD), f32),
            pltpu.VMEM((3, SIDE * T // 3, 3 * SIDE * T), f32),
            pltpu.VMEM((SIDE * T, 2 * HD), f32),
            pltpu.VMEM((SIDE,) + block, bf),
            pltpu.VMEM((SIDE,) + block, bf),
            pltpu.VMEM((SIDE,) + block, bf),
            pltpu.VMEM((SIDE, 8, 256), f32),
            pltpu.VMEM((SIDE, 8, 256), f32),
            pltpu.VMEM((8, HD), f32),
            dma((9,)),
            dma((9,)),
            dma((3, SIDE)),
            dma((2,)),
            dma((9,)),
        ],
        compiler_params=pltpu.CompilerParams(
            collective_id=0, has_side_effects=True, vmem_limit_bytes=48 * 1024 * 1024
        ),
        name="clip_attention",
    )(*[pltpu.with_memory_space_constraint(a, pltpu.HBM) for a in (
        queries, keys, values, gain_q, gain_k, clip_ids[None, :], jnp.asarray(freq), clip_grid.T,
    )])


def solution(mesh):
    in_specs = (
        P(("batch", "ctx"), "row"),
        P(("batch", "ctx"), "row"),
        P(("batch", "ctx"), "row"),
        P("row"),
        P("row"),
        P(("batch", "ctx")),
        P("batch", None),
    )
    out_specs = P(("batch", "ctx"), "row")
    return jax.shard_map(
        functools.partial(on_device, mesh.shape["row"]),
        mesh=mesh, in_specs=in_specs, out_specs=out_specs, check_vma=False,
    )
```

```python
import functools
import math

import jax
import jax.numpy as jnp
import numpy as np
from jax import lax
from jax.experimental import pallas as pl
from jax.experimental.pallas import tpu as pltpu
from jax.sharding import PartitionSpec as P

HD = 128
CLIPS = 4
EPSILON = 1e-06
NEGATIVE = -1e30
ROTARY_BASE = 10000.0
LOG2E = math.log2(math.e)
SIDE = 4
MESH = pl.DeviceIdType.MESH


def frequencies():
    p = HD // 6
    f = HD - 4 * p
    base = np.float32(ROTARY_BASE)
    first = np.float32(1.0) / base ** (np.arange(0, f, 2, dtype=np.float32) / np.float32(f))
    other = np.float32(1.0) / base ** (np.arange(0, 2 * p, 2, dtype=np.float32) / np.float32(2 * p))
    return np.repeat(np.concatenate([first, other, other]), 2)[None, :].astype(np.float32), f, f + 2 * p


def cols(h):
    if isinstance(h, int):
        return pl.ds(h * HD, HD)
    return pl.ds(pl.multiple_of(h * HD, HD), HD)


def kernel(
    rows_n, model, cut_a, cut_b,
    q_hbm, k_hbm, v, gq_hbm, gk_hbm, ids_hbm, freq_hbm, grid_hbm, out,
    q, k, gq, gk, ids, freq, grid, pad, ssq_send, ssq_recv, cz_send, cz_recv, cx_send, cx_recv,
    krot, qrot, kh, vh, k4, v4, qh, q4, m_scr, s_scr, a_scr, o_send, o4_send, o4_recv, st_send, st_recv, starts_scr,
    sem_s, sem_r, sem_zr, sem_xr, sem_in,
):
    T = q.shape[0]
    me = lax.axis_index("ctx")
    row = lax.axis_index("row")
    x = me // SIDE
    z = lax.rem(me, SIDE)
    zs = [lax.rem(z + d, SIDE) for d in range(SIDE)]
    xs = [lax.rem(x + d, SIDE) for d in range(SIDE)]
    zpeer = [x * SIDE + a for a in zs]
    xpeer = [a * SIDE + z for a in xs]
    zsrc = [lax.rem(z + SIDE - d, SIDE) for d in range(SIDE)]
    xsrc = [lax.rem(x + SIDE - d, SIDE) for d in range(SIDE)]
    scale = 1.0 / math.sqrt(HD)
    wide = SIDE * T

    def left(ref, i):
        return ref.at[i, :, 0:HD]

    barrier = pltpu.get_barrier_semaphore()
    for d in range(1, SIDE):
        pl.semaphore_signal(barrier, inc=1, device_id={"ctx": zpeer[d]}, device_id_type=MESH)
        pl.semaphore_signal(barrier, inc=1, device_id={"ctx": xpeer[d]}, device_id_type=MESH)
    for d in range(1, rows_n):
        pl.semaphore_signal(
            barrier, inc=1, device_id={"row": lax.rem(row + d, rows_n)}, device_id_type=MESH
        )
    loads = [
        pltpu.make_async_copy(src, dst, sem_in.at[i])
        for i, (src, dst) in enumerate([
            (ids_hbm, ids), (q_hbm, q), (k_hbm, k), (grid_hbm, grid), (freq_hbm, freq),
            (gk_hbm, gk), (gq_hbm, gq), (v.at[:, cols(z)], left(vh, z)), (v.at[:, cols(4)], left(v4, z)),
        ])
    ]
    for c in loads:
        c.start()

    def send(src, dst, group, arrival, where):
        pltpu.make_async_remote_copy(
            src_ref=src, dst_ref=dst, send_sem=sem_s.at[group], recv_sem=arrival, device_id=where,
            device_id_type=MESH,
        ).start()

    def done(ref, sem):
        pltpu.make_async_copy(ref, ref, sem).wait()

    def to_z(n, src, dst):
        for d in (1, 3, 2):
            send(src.at[:, cols(zs[d])], dst, 2 + n, sem_zr.at[n, d], {"ctx": zpeer[d]})

    def four_to_z(n, src, dst):
        for d in (1, 3, 2):
            send(src.at[:, cols(4)], left(dst, z), 2 + n, sem_r.at[n], {"ctx": zpeer[d]})

    def to_near(n, src, dst, a):
        for g, d in ((1, 1), (2, 3)):
            send(src, left(dst, g * SIDE + a), n, sem_xr.at[n, 0], {"ctx": xpeer[d]})

    def to_far(n, src, dst, a):
        send(src, left(dst, 3 * SIDE + a), n, sem_xr.at[n, 1], {"ctx": xpeer[2]})

    loads[0].wait()
    level = lax.broadcasted_iota(jnp.int32, (8, T), 0)
    below = jnp.where(jnp.broadcast_to(ids[...], (8, T)) < level, 1.0, 0.0).astype(jnp.float32)
    cz_send[...] = jnp.broadcast_to(jnp.sum(below, axis=1, keepdims=True), (8, HD))

    with jax.named_scope("entry_wait"):
        pl.semaphore_wait(barrier, 2 * (SIDE - 1) + rows_n - 1)

    for d in range(1, SIDE):
        send(cz_send, cz_recv.at[d], 6, sem_r.at[3], {"ctx": zpeer[d]})
    to_z(0, v, left(vh, z))
    to_near(0, v.at[:, cols(z)], vh, z)
    to_far(0, v.at[:, cols(z)], vh, z)

    with jax.named_scope("squares"):
        pad[T:256, :] = jnp.zeros((256 - T, HD), jnp.float32)
        ssq_send[...] = jnp.zeros_like(ssq_send)
        for i, ref in enumerate((q, k)):
            loads[1 + i].wait()
            acc = None
            for h in range(5):
                w = ref[:, h * HD : (h + 1) * HD].astype(jnp.float32)
                acc = w * w if acc is None else acc + w * w
            pad[:T, :] = acc
            ssq_send[i : i + 1, :] = jnp.sum(jnp.transpose(pad[0:256, :]), axis=0, keepdims=True)
    for d in range(1, rows_n):
        send(
            ssq_send, ssq_recv.at[d], 7, sem_r.at[5], {"row": lax.rem(row + d, rows_n)}
        )

    with jax.named_scope("count_z_wait"):
        done(cz_recv.at[1:SIDE], sem_r.at[3])
    part = cz_send[...]
    for d in range(1, SIDE):
        part = part + cz_recv[d]
    cx_send[...] = part
    for d in range(1, SIDE):
        send(cx_send, cx_recv.at[d], 6, sem_r.at[4], {"ctx": xpeer[d]})

    def forward(n, ref, j):
        slot = left(ref, zsrc[j])
        with jax.named_scope("%s_wait%d" % ("vk"[n], j)):
            done(slot, sem_zr.at[n, j])
        to_near(n, slot, ref, zsrc[j])
        if n == 0:
            to_far(n, slot, ref, zsrc[j])

    four_to_z(0, v, v4)
    forward(0, vh, 1)
    forward(0, vh, 3)
    with jax.named_scope("count_x_wait"):
        done(cx_recv.at[1:SIDE], sem_r.at[4])
    starts = cx_send[...]
    for d in range(1, SIDE):
        starts = starts + cx_recv[d]
    starts_scr[...] = starts

    for c in loads[3:]:
        c.wait()
    lane = lax.broadcasted_iota(jnp.int32, (T, HD), 1)
    token = (lax.broadcasted_iota(jnp.int32, (T, HD), 0) + me * T).astype(jnp.float32)
    first = jnp.zeros((T, HD), jnp.float32)
    shape_of = grid[...].astype(jnp.float32)
    height = jnp.broadcast_to(shape_of[0:1, 0:1], (T, HD))
    width = jnp.broadcast_to(shape_of[1:2, 0:1], (T, HD))
    for c in range(1, CLIPS):
        s = jnp.broadcast_to(starts[c : c + 1, :], (T, HD))
        inside = token >= s
        first = jnp.where(inside, s, first)
        height = jnp.where(inside, shape_of[0:1, c : c + 1], height)
        width = jnp.where(inside, shape_of[1:2, c : c + 1], width)
    offset = token - first
    frame = jnp.floor((offset + 0.5) / (height * width))
    lines = jnp.floor((offset + 0.5) / width)
    line = lines - height * jnp.floor((lines + 0.5) / height)
    column = offset - width * lines
    place = jnp.where(lane < cut_a, frame, jnp.where(lane < cut_b, line, column))
    angle = place * freq[...]
    with jax.named_scope("trig"):
        cosine = jnp.cos(angle)
    even = lax.rem(lane, 2) == 0
    sine = jnp.sin(angle)

    with jax.named_scope("square_wait"):
        if rows_n > 1:
            done(ssq_recv.at[1:rows_n], sem_r.at[5])
    total = ssq_send[...]
    for d in range(1, rows_n):
        total = total + ssq_recv[d]
    rs = lax.rsqrt(total / model + EPSILON)

    def rope(src, dst, gain, i):
        col = jnp.transpose(jnp.broadcast_to(rs[i : i + 1, :], (HD, rs.shape[1])))[:T, :]
        for h in (4, 0, 1, 2, 3):
            a = src[:, h * HD : (h + 1) * HD].astype(jnp.float32) * col
            a = a * gain[h * HD : (h + 1) * HD].reshape(1, HD)
            partner = jnp.where(even, -pltpu.roll(a, HD - 1, 1), pltpu.roll(a, 1, 1))
            dst[:, h * HD : (h + 1) * HD] = (a * cosine + partner * sine).astype(jnp.bfloat16)

    with jax.named_scope("rope_k"):
        rope(k, krot, gk, 1)
    to_z(1, krot, left(kh, z))
    to_near(1, krot.at[:, cols(z)], kh, z)
    to_far(1, krot.at[:, cols(z)], kh, z)
    forward(0, vh, 2)
    with jax.named_scope("rope_q"):
        rope(q, qrot, gq, 0)
    for d in (1, 3, 2):
        send(qrot.at[:, cols(zs[d])], left(qh, z), 4, sem_zr.at[2, d], {"ctx": zpeer[d]})
    kh[z, :, 0:HD] = krot[:, cols(z)]
    k4[z, :, 0:HD] = krot[:, cols(4)]
    qh[z, :, 0:HD] = qrot[:, cols(z)]
    q4[x, :, 0:HD] = qrot[:, cols(4)]

    lanes = lax.broadcasted_iota(jnp.int32, (T, HD), 1)

    def member(first_token, inside, outside):
        t = (lax.broadcasted_iota(jnp.int32, (T, HD), 0) + first_token).astype(jnp.float32)
        c = jnp.zeros((T, HD), jnp.int32)
        for i in range(1, CLIPS):
            c = c + jnp.where(t >= starts_scr[i : i + 1, :], 1, 0)
        value = jnp.where(c == lanes, inside, outside)
        return jnp.where(lanes < CLIPS, value, 0.0).astype(jnp.bfloat16)

    ones = jnp.ones((T, HD), jnp.bfloat16)

    def fill(g, d):
        def body(i, carry):
            vh[g * SIDE + i, :, HD:] = ones
            kh[g * SIDE + i, :, HD:] = member((xsrc[d] * SIDE + i) * T, 1.0, 0.0)
            return carry

        lax.fori_loop(0, SIDE, body, 0)

    def fill_four(i, carry):
        v4[i, :, HD:] = ones
        k4[i, :, HD:] = member((x * SIDE + i) * T, 1.0, 0.0)
        qh[i, :, HD:] = member((x * SIDE + i) * T, 0.0, NEGATIVE)
        q4[i, :, HD:] = member((i * SIDE + z) * T, 0.0, NEGATIVE)
        return carry

    with jax.named_scope("fill"):
        lax.fori_loop(0, SIDE, fill_four, 0)
        for g, d in enumerate((0, 1, 3, 2)):
            fill(g, d)
    for j in (1, 3, 2):
        forward(1, kh, j)
    for j in (1, 3, 2):
        to_far(1, left(kh, zsrc[j]), kh, zsrc[j])
    for d in (1, 3, 2):
        send(qrot.at[:, cols(4)], left(q4, x), 4, sem_r.at[2], {"ctx": xpeer[d]})

    third = wide // 3

    def attend(queries, keys, vals, carried=None):
        keys = keys.reshape(-1, 2 * HD)
        vals = vals.reshape(-1, 2 * HD)
        n = keys.shape[0]
        for t in range(3):
            tile = pl.ds(t * third, third)
            s = lax.dot_general(
                queries[t * third : (t + 1) * third], keys, (((1,), (1,)), ((), ())),
                preferred_element_type=jnp.float32,
            )
            s_scr[t, :, 0:n] = s
            m = jnp.max(s, axis=1, keepdims=True)
            if carried:
                old = m_scr[tile, 0:1]
                m = jnp.maximum(m, old)
                factor = jnp.exp2((old - m) * (scale * LOG2E))
            w = jnp.exp2((s_scr[t, :, 0:n] - m) * (scale * LOG2E)).astype(jnp.bfloat16)
            o = jnp.dot(w, vals, preferred_element_type=jnp.float32)
            if carried:
                o = o + a_scr[tile, :] * factor
            a_scr[tile, :] = o
            m_scr[tile, :] = jnp.broadcast_to(m, (third, HD))

    def divide(o):
        return (o[:, :HD] / o[:, HD:]).astype(jnp.bfloat16)

    with jax.named_scope("q_wait"):
        for n in (3, 1, 2):
            done(left(qh, zs[n]), sem_zr.at[2, SIDE - n])
    four_to_z(1, krot, k4)
    with jax.named_scope("own_attend"):
        attend(qh[...].reshape(wide, 2 * HD), kh[0:SIDE], vh[0:SIDE])
    queries = qh[...].reshape(wide, 2 * HD)
    for name, side, first, last in (("near", 0, SIDE, 3 * SIDE), ("far", 1, 3 * SIDE, 4 * SIDE)):
        with jax.named_scope(name + "_wait"):
            done(left(vh, pl.ds(first, last - first)), sem_xr.at[0, side])
            done(left(kh, pl.ds(first, last - first)), sem_xr.at[1, side])
        with jax.named_scope(name + "_attend"):
            attend(queries, kh[first:last], vh[first:last], True)
    with jax.named_scope("divide"):
        o_send[...] = divide(a_scr[...]).reshape(SIDE, T, HD)
    for n in (2, 1, 3):
        send(o_send.at[zs[n]], out.at[:, cols(z)], 5, sem_r.at[6], {"ctx": zpeer[n]})
    out[:, cols(z)] = o_send[z]

    with jax.named_scope("four_wait"):
        done(left(v4, pl.ds(0, SIDE - 1)), sem_r.at[0])
        done(left(k4, pl.ds(0, SIDE - 1)), sem_r.at[1])
        done(left(q4, pl.ds(0, SIDE - 1)), sem_r.at[2])
    with jax.named_scope("four_attend"):
        pad[wide:, :] = jnp.zeros((64, HD), jnp.float32)
        attend(q4[...].reshape(wide, 2 * HD), k4[...], v4[...])
        m, o = m_scr[...], a_scr[...]
        o4_send[...] = divide(o).reshape(SIDE, T, HD)
        flags = lax.broadcasted_iota(jnp.int32, (wide, HD), 1)
        pad[0:wide, :] = jnp.where(flags == 0, m * scale, jnp.where(flags == 1, o[:, HD:], 0.0))
        for i in range(SIDE):
            st_send[i] = jnp.transpose(pad[i * T : i * T + 256, :])[:8, :]
    for d in (1, 3, 2):
        send(o4_send.at[xs[d]], o4_recv.at[x], 5, sem_r.at[7], {"ctx": xpeer[d]})
        send(st_send.at[xs[d]], st_recv.at[x], 8, sem_r.at[8], {"ctx": xpeer[d]})
    o4_recv[x] = o4_send[x]
    st_recv[x] = st_send[x]
    with jax.named_scope("four_back_wait"):
        done(o4_recv.at[0 : SIDE - 1], sem_r.at[7])
        done(st_recv.at[0 : SIDE - 1], sem_r.at[8])
    peaks = [st_recv[i, 0:1, :] for i in range(SIDE)]
    peak = functools.reduce(jnp.maximum, peaks)
    shares = [st_recv[i, 1:2, :] * jnp.exp(peaks[i] - peak) for i in range(SIDE)]
    whole = functools.reduce(jnp.add, shares)
    line = lax.broadcasted_iota(jnp.int32, (HD, st_recv.shape[2]), 0)
    table = jnp.zeros((HD, st_recv.shape[2]), jnp.float32)
    for i in range(SIDE):
        table = jnp.where(line == i, shares[i] / whole, table)
    share = jnp.transpose(table)[:T, :]
    num = jnp.zeros((T, HD), jnp.float32)
    for i in range(SIDE):
        num = num + share[:, i : i + 1] * o4_recv[i].astype(jnp.float32)
    out[:, cols(4)] = num.astype(jnp.bfloat16)

    with jax.named_scope("back_wait"):
        done(o4_recv.at[0 : SIDE - 1], sem_r.at[6])
    with jax.named_scope("send_wait"):
        done(left(vh, pl.ds(0, 3 * SIDE)), sem_s.at[0])
        done(left(kh, pl.ds(0, 3 * SIDE)), sem_s.at[1])
        for group in range(2, 6):
            done(left(vh, pl.ds(0, 6)), sem_s.at[group])
        done(st_recv.at[0 : SIDE - 1], sem_s.at[6])
        if rows_n > 1:
            done(ssq_recv.at[1:rows_n], sem_s.at[7])
        done(st_recv.at[0 : SIDE - 1], sem_s.at[8])


def on_device(rows_n, queries, keys, values, gain_q, gain_k, clip_ids, clip_grid):
    T, width = queries.shape
    freq, cut_a, cut_b = frequencies()
    bf, f32 = jnp.bfloat16, jnp.float32
    vm = pl.BlockSpec(memory_space=pltpu.VMEM)
    dma = pltpu.SemaphoreType.DMA
    block = (T, HD)
    return pl.pallas_call(
        functools.partial(kernel, rows_n, float(width * rows_n), cut_a, cut_b),
        out_shape=pltpu.VMEM((T, width), bf),
        in_specs=[pl.BlockSpec(memory_space=pltpu.HBM)] * 8,
        out_specs=vm,
        scratch_shapes=[
            pltpu.VMEM((T, width), bf),
            pltpu.VMEM((T, width), bf),
            pltpu.VMEM((width,), f32),
            pltpu.VMEM((width,), f32),
            pltpu.VMEM((1, T), jnp.int32),
            pltpu.VMEM((1, HD), f32),
            pltpu.VMEM((2, CLIPS), jnp.int32),
            pltpu.VMEM((SIDE * T + 64, HD), f32),
            pltpu.VMEM((8, 256), f32),
            pltpu.VMEM((rows_n, 8, 256), f32),
            pltpu.VMEM((8, HD), f32),
            pltpu.VMEM((SIDE, 8, HD), f32),
            pltpu.VMEM((8, HD), f32),
            pltpu.VMEM((SIDE, 8, HD), f32),
            pltpu.VMEM((T, width), bf),
            pltpu.VMEM((T, width), bf),
            pltpu.VMEM((SIDE * SIDE, T, 2 * HD), bf),
            pltpu.VMEM((SIDE * SIDE, T, 2 * HD), bf),
            pltpu.VMEM((SIDE, T, 2 * HD), bf),
            pltpu.VMEM((SIDE, T, 2 * HD), bf),
            pltpu.VMEM((SIDE, T, 2 * HD), bf),
            pltpu.VMEM((SIDE, T, 2 * HD), bf),
            pltpu.VMEM((SIDE * T, HD), f32),
            pltpu.VMEM((3, SIDE * T // 3, 2 * SIDE * T), f32),
            pltpu.VMEM((SIDE * T, 2 * HD), f32),
            pltpu.VMEM((SIDE,) + block, bf),
            pltpu.VMEM((SIDE,) + block, bf),
            pltpu.VMEM((SIDE,) + block, bf),
            pltpu.VMEM((SIDE, 8, 256), f32),
            pltpu.VMEM((SIDE, 8, 256), f32),
            pltpu.VMEM((8, HD), f32),
            dma((9,)),
            dma((9,)),
            dma((3, SIDE)),
            dma((2, 2)),
            dma((9,)),
        ],
        compiler_params=pltpu.CompilerParams(
            collective_id=0, has_side_effects=True, vmem_limit_bytes=48 * 1024 * 1024
        ),
        name="clip_attention",
    )(*[pltpu.with_memory_space_constraint(a, pltpu.HBM) for a in (
        queries, keys, values, gain_q, gain_k, clip_ids[None, :], jnp.asarray(freq), clip_grid.T,
    )])


def solution(mesh):
    in_specs = (
        P(("batch", "ctx"), "row"),
        P(("batch", "ctx"), "row"),
        P(("batch", "ctx"), "row"),
        P("row"),
        P("row"),
        P(("batch", "ctx")),
        P("batch", None),
    )
    out_specs = P(("batch", "ctx"), "row")
    return jax.shard_map(
        functools.partial(on_device, mesh.shape["row"]),
        mesh=mesh, in_specs=in_specs, out_specs=out_specs, check_vma=False,
    )
```

```python
import functools
import math

import jax
import jax.numpy as jnp
import numpy as np
from jax import lax
from jax.experimental import pallas as pl
from jax.experimental.pallas import tpu as pltpu
from jax.sharding import PartitionSpec as P

HD = 128
CLIPS = 4
EPSILON = 1e-06
NEGATIVE = -1e30
ROTARY_BASE = 10000.0
LOG2E = math.log2(math.e)
SIDE = 4
MESH = pl.DeviceIdType.MESH


def frequencies():
    p = HD // 6
    f = HD - 4 * p
    base = np.float32(ROTARY_BASE)
    first = np.float32(1.0) / base ** (np.arange(0, f, 2, dtype=np.float32) / np.float32(f))
    other = np.float32(1.0) / base ** (np.arange(0, 2 * p, 2, dtype=np.float32) / np.float32(2 * p))
    return np.repeat(np.concatenate([first, other, other]), 2)[None, :].astype(np.float32), f, f + 2 * p


def cols(h):
    if isinstance(h, int):
        return pl.ds(h * HD, HD)
    return pl.ds(pl.multiple_of(h * HD, HD), HD)


def kernel(
    rows_n, model, cut_a, cut_b,
    q_hbm, k_hbm, v, gq_hbm, gk_hbm, ids_hbm, freq_hbm, grid_hbm, out,
    q, k, gq, gk, ids, freq, grid, pad, ssq_send, ssq_recv, cz_send, cz_recv, cx_send, cx_recv,
    krot, qrot, kh, vh, k4, v4, qh, q4, m_scr, s_scr, a_scr, o_send, o4_send, o4_recv, st_send, st_recv, starts_scr,
    sem_s, sem_r, sem_zr, sem_xr, sem_in,
):
    T = q.shape[0]
    me = lax.axis_index("ctx")
    row = lax.axis_index("row")
    x = me // SIDE
    z = lax.rem(me, SIDE)
    zs = [lax.rem(z + d, SIDE) for d in range(SIDE)]
    xs = [lax.rem(x + d, SIDE) for d in range(SIDE)]
    zpeer = [x * SIDE + a for a in zs]
    xpeer = [a * SIDE + z for a in xs]
    zsrc = [lax.rem(z + SIDE - d, SIDE) for d in range(SIDE)]
    xsrc = [lax.rem(x + SIDE - d, SIDE) for d in range(SIDE)]
    scale = 1.0 / math.sqrt(HD)
    wide = SIDE * T

    def left(ref, i):
        return ref.at[i, :, 0:HD]

    loads = [
        pltpu.make_async_copy(src, dst, sem_in.at[i])
        for i, (src, dst) in enumerate([
            (ids_hbm, ids), (q_hbm, q), (k_hbm, k), (grid_hbm, grid), (freq_hbm, freq),
            (gk_hbm, gk), (gq_hbm, gq), (v.at[:, cols(z)], left(vh, z)), (v.at[:, cols(4)], left(v4, z)),
        ])
    ]
    loads[0].start()
    barrier = pltpu.get_barrier_semaphore()
    for d in range(1, SIDE):
        pl.semaphore_signal(barrier, inc=1, device_id={"ctx": zpeer[d]}, device_id_type=MESH)
        pl.semaphore_signal(barrier, inc=1, device_id={"ctx": xpeer[d]}, device_id_type=MESH)
    for d in range(1, rows_n):
        pl.semaphore_signal(
            barrier, inc=1, device_id={"row": lax.rem(row + d, rows_n)}, device_id_type=MESH
        )
    for c in loads[1:]:
        c.start()

    def send(src, dst, group, arrival, where):
        pltpu.make_async_remote_copy(
            src_ref=src, dst_ref=dst, send_sem=sem_s.at[group], recv_sem=arrival, device_id=where,
            device_id_type=MESH,
        ).start()

    def done(ref, sem):
        pltpu.make_async_copy(ref, ref, sem).wait()

    def to_z(n, src, dst):
        for d in (1, 3, 2):
            send(src.at[:, cols(zs[d])], dst, 2 + n, sem_zr.at[n, d], {"ctx": zpeer[d]})

    def four_to_z(n, src, dst):
        for d in (1, 3, 2):
            send(src.at[:, cols(4)], left(dst, z), 2 + n, sem_r.at[n], {"ctx": zpeer[d]})

    def to_near(n, src, dst, a):
        for g, d in ((1, 1), (2, 3)):
            send(src, left(dst, g * SIDE + a), n, sem_xr.at[n, 0], {"ctx": xpeer[d]})

    def to_far(n, src, dst, a):
        send(src, left(dst, 3 * SIDE + a), n, sem_xr.at[n, 1], {"ctx": xpeer[2]})

    loads[0].wait()
    level = lax.broadcasted_iota(jnp.int32, (8, T), 0)
    below = jnp.where(jnp.broadcast_to(ids[...], (8, T)) < level, 1.0, 0.0).astype(jnp.float32)
    cz_send[...] = jnp.broadcast_to(jnp.sum(below, axis=1, keepdims=True), (8, HD))

    with jax.named_scope("entry_wait"):
        pl.semaphore_wait(barrier, 2 * (SIDE - 1) + rows_n - 1)

    for d in range(1, SIDE):
        send(cz_send, cz_recv.at[d], 6, sem_r.at[3], {"ctx": zpeer[d]})
    to_z(0, v, left(vh, z))
    to_near(0, v.at[:, cols(z)], vh, z)
    to_far(0, v.at[:, cols(z)], vh, z)

    with jax.named_scope("squares"):
        pad[T:256, :] = jnp.zeros((256 - T, HD), jnp.float32)
        ssq_send[...] = jnp.zeros_like(ssq_send)
        for i, ref in enumerate((q, k)):
            loads[1 + i].wait()
            acc = None
            for h in range(5):
                w = ref[:, h * HD : (h + 1) * HD].astype(jnp.float32)
                acc = w * w if acc is None else acc + w * w
            pad[:T, :] = acc
            ssq_send[i : i + 1, :] = jnp.sum(jnp.transpose(pad[0:256, :]), axis=0, keepdims=True)
    for d in range(1, rows_n):
        send(
            ssq_send, ssq_recv.at[d], 7, sem_r.at[5], {"row": lax.rem(row + d, rows_n)}
        )

    with jax.named_scope("count_z_wait"):
        done(cz_recv.at[1:SIDE], sem_r.at[3])
    part = cz_send[...]
    for d in range(1, SIDE):
        part = part + cz_recv[d]
    cx_send[...] = part
    for d in range(1, SIDE):
        send(cx_send, cx_recv.at[d], 6, sem_r.at[4], {"ctx": xpeer[d]})

    def forward(n, ref, j):
        slot = left(ref, zsrc[j])
        with jax.named_scope("%s_wait%d" % ("vk"[n], j)):
            done(slot, sem_zr.at[n, j])
        to_near(n, slot, ref, zsrc[j])
        if n == 0:
            to_far(n, slot, ref, zsrc[j])

    four_to_z(0, v, v4)
    forward(0, vh, 1)
    forward(0, vh, 3)
    with jax.named_scope("count_x_wait"):
        done(cx_recv.at[1:SIDE], sem_r.at[4])
    starts = cx_send[...]
    for d in range(1, SIDE):
        starts = starts + cx_recv[d]
    starts_scr[...] = starts

    for c in loads[3:]:
        c.wait()
    lane = lax.broadcasted_iota(jnp.int32, (T, HD), 1)
    token = (lax.broadcasted_iota(jnp.int32, (T, HD), 0) + me * T).astype(jnp.float32)
    first = jnp.zeros((T, HD), jnp.float32)
    shape_of = grid[...].astype(jnp.float32)
    height = jnp.broadcast_to(shape_of[0:1, 0:1], (T, HD))
    width = jnp.broadcast_to(shape_of[1:2, 0:1], (T, HD))
    for c in range(1, CLIPS):
        s = jnp.broadcast_to(starts[c : c + 1, :], (T, HD))
        inside = token >= s
        first = jnp.where(inside, s, first)
        height = jnp.where(inside, shape_of[0:1, c : c + 1], height)
        width = jnp.where(inside, shape_of[1:2, c : c + 1], width)
    offset = token - first
    frame = jnp.floor((offset + 0.5) / (height * width))
    lines = jnp.floor((offset + 0.5) / width)
    line = lines - height * jnp.floor((lines + 0.5) / height)
    column = offset - width * lines
    place = jnp.where(lane < cut_a, frame, jnp.where(lane < cut_b, line, column))
    angle = place * freq[...]
    with jax.named_scope("trig"):
        cosine = jnp.cos(angle)
    even = lax.rem(lane, 2) == 0
    sine = jnp.sin(angle)

    with jax.named_scope("square_wait"):
        if rows_n > 1:
            done(ssq_recv.at[1:rows_n], sem_r.at[5])
    total = ssq_send[...]
    for d in range(1, rows_n):
        total = total + ssq_recv[d]
    rs = lax.rsqrt(total / model + EPSILON)

    def rope(src, dst, gain, i):
        col = jnp.transpose(jnp.broadcast_to(rs[i : i + 1, :], (HD, rs.shape[1])))[:T, :]
        for h in (4, 0, 1, 2, 3):
            a = src[:, h * HD : (h + 1) * HD].astype(jnp.float32) * col
            a = a * gain[h * HD : (h + 1) * HD].reshape(1, HD)
            partner = jnp.where(even, -pltpu.roll(a, HD - 1, 1), pltpu.roll(a, 1, 1))
            dst[:, h * HD : (h + 1) * HD] = (a * cosine + partner * sine).astype(jnp.bfloat16)

    with jax.named_scope("rope_k"):
        rope(k, krot, gk, 1)
    to_z(1, krot, left(kh, z))
    to_near(1, krot.at[:, cols(z)], kh, z)
    to_far(1, krot.at[:, cols(z)], kh, z)
    forward(0, vh, 2)
    with jax.named_scope("rope_q"):
        rope(q, qrot, gq, 0)
    for d in (1, 3, 2):
        send(qrot.at[:, cols(zs[d])], left(qh, z), 4, sem_zr.at[2, d], {"ctx": zpeer[d]})
    kh[z, :, 0:HD] = krot[:, cols(z)]
    k4[z, :, 0:HD] = krot[:, cols(4)]
    qh[z, :, 0:HD] = qrot[:, cols(z)]
    q4[x, :, 0:HD] = qrot[:, cols(4)]

    lanes = lax.broadcasted_iota(jnp.int32, (T, HD), 1)

    def member(first_token, inside, outside):
        t = (lax.broadcasted_iota(jnp.int32, (T, HD), 0) + first_token).astype(jnp.float32)
        c = jnp.zeros((T, HD), jnp.int32)
        for i in range(1, CLIPS):
            c = c + jnp.where(t >= starts_scr[i : i + 1, :], 1, 0)
        value = jnp.where(c == lanes, inside, outside)
        return jnp.where(lanes < CLIPS, value, 0.0).astype(jnp.bfloat16)

    ones = jnp.ones((T, HD), jnp.bfloat16)

    def fill(g, d):
        def body(i, carry):
            vh[g * SIDE + i, :, HD:] = ones
            kh[g * SIDE + i, :, HD:] = member((xsrc[d] * SIDE + i) * T, 1.0, 0.0)
            return carry

        lax.fori_loop(0, SIDE, body, 0)

    def fill_four(i, carry):
        v4[i, :, HD:] = ones
        k4[i, :, HD:] = member((x * SIDE + i) * T, 1.0, 0.0)
        qh[i, :, HD:] = member((x * SIDE + i) * T, 0.0, NEGATIVE)
        q4[i, :, HD:] = member((i * SIDE + z) * T, 0.0, NEGATIVE)
        return carry

    with jax.named_scope("fill"):
        lax.fori_loop(0, SIDE, fill_four, 0)
        for g, d in enumerate((0, 1, 3, 2)):
            fill(g, d)
    for j in (1, 3, 2):
        forward(1, kh, j)
    for j in (1, 3, 2):
        to_far(1, left(kh, zsrc[j]), kh, zsrc[j])
    for d in (1, 3, 2):
        send(qrot.at[:, cols(4)], left(q4, x), 4, sem_r.at[2], {"ctx": xpeer[d]})

    third = wide // 3

    def attend(queries, keys, vals, carried=None):
        keys = keys.reshape(-1, 2 * HD)
        vals = vals.reshape(-1, 2 * HD)
        n = keys.shape[0]
        for t in range(3):
            tile = pl.ds(t * third, third)
            s = lax.dot_general(
                queries[t * third : (t + 1) * third], keys, (((1,), (1,)), ((), ())),
                preferred_element_type=jnp.float32,
            )
            s_scr[t, :, 0:n] = s
            m = jnp.max(s, axis=1, keepdims=True)
            if carried:
                old = m_scr[tile, 0:1]
                m = jnp.maximum(m, old)
                factor = jnp.exp2((old - m) * (scale * LOG2E))
            w = jnp.exp2((s_scr[t, :, 0:n] - m) * (scale * LOG2E)).astype(jnp.bfloat16)
            o = jnp.dot(w, vals, preferred_element_type=jnp.float32)
            if carried:
                o = o + a_scr[tile, :] * factor
            a_scr[tile, :] = o
            m_scr[tile, :] = jnp.broadcast_to(m, (third, HD))

    def divide(o):
        return (o[:, :HD] / o[:, HD:]).astype(jnp.bfloat16)

    with jax.named_scope("q_wait"):
        for n in (3, 1, 2):
            done(left(qh, zs[n]), sem_zr.at[2, SIDE - n])
    four_to_z(1, krot, k4)
    with jax.named_scope("own_attend"):
        attend(qh[...].reshape(wide, 2 * HD), kh[0:SIDE], vh[0:SIDE])
    queries = qh[...].reshape(wide, 2 * HD)
    for name, side, first, last in (("near", 0, SIDE, 3 * SIDE), ("far", 1, 3 * SIDE, 4 * SIDE)):
        with jax.named_scope(name + "_wait"):
            done(left(vh, pl.ds(first, last - first)), sem_xr.at[0, side])
            done(left(kh, pl.ds(first, last - first)), sem_xr.at[1, side])
        with jax.named_scope(name + "_attend"):
            attend(queries, kh[first:last], vh[first:last], True)
    with jax.named_scope("divide"):
        o_send[...] = divide(a_scr[...]).reshape(SIDE, T, HD)
    for n in (2, 1, 3):
        send(o_send.at[zs[n]], out.at[:, cols(z)], 5, sem_r.at[6], {"ctx": zpeer[n]})
    out[:, cols(z)] = o_send[z]

    with jax.named_scope("four_wait"):
        done(left(v4, pl.ds(0, SIDE - 1)), sem_r.at[0])
        done(left(k4, pl.ds(0, SIDE - 1)), sem_r.at[1])
        done(left(q4, pl.ds(0, SIDE - 1)), sem_r.at[2])
    with jax.named_scope("four_attend"):
        pad[wide:, :] = jnp.zeros((64, HD), jnp.float32)
        attend(q4[...].reshape(wide, 2 * HD), k4[...], v4[...])
        o4_send[...] = divide(a_scr[...]).reshape(SIDE, T, HD)
    for d in (2, 1, 3):
        send(o4_send.at[xs[d]], o4_recv.at[x], 5, sem_r.at[7], {"ctx": xpeer[d]})
    with jax.named_scope("stats"):
        flags = lax.broadcasted_iota(jnp.int32, (wide, HD), 1)
        pad[0:wide, :] = jnp.where(
            flags == 0, m_scr[...] * scale, jnp.where(flags == 1, a_scr[:, HD:], 0.0)
        )
        for i in range(SIDE):
            st_send[i] = jnp.transpose(pad[i * T : i * T + 256, :])[:8, :]
    for d in (2, 1, 3):
        send(st_send.at[xs[d]], st_recv.at[x], 8, sem_r.at[8], {"ctx": xpeer[d]})
    o4_recv[x] = o4_send[x]
    st_recv[x] = st_send[x]
    with jax.named_scope("four_back_wait"):
        done(o4_recv.at[0 : SIDE - 1], sem_r.at[7])
        done(st_recv.at[0 : SIDE - 1], sem_r.at[8])
    peaks = [st_recv[i, 0:1, :] for i in range(SIDE)]
    peak = functools.reduce(jnp.maximum, peaks)
    shares = [st_recv[i, 1:2, :] * jnp.exp(peaks[i] - peak) for i in range(SIDE)]
    whole = functools.reduce(jnp.add, shares)
    line = lax.broadcasted_iota(jnp.int32, (HD, st_recv.shape[2]), 0)
    table = jnp.zeros((HD, st_recv.shape[2]), jnp.float32)
    for i in range(SIDE):
        table = jnp.where(line == i, shares[i] / whole, table)
    share = jnp.transpose(table)[:T, :]
    num = jnp.zeros((T, HD), jnp.float32)
    for i in range(SIDE):
        num = num + share[:, i : i + 1] * o4_recv[i].astype(jnp.float32)
    out[:, cols(4)] = num.astype(jnp.bfloat16)

    with jax.named_scope("back_wait"):
        done(o4_recv.at[0 : SIDE - 1], sem_r.at[6])
    with jax.named_scope("send_wait"):
        done(left(vh, pl.ds(0, 3 * SIDE)), sem_s.at[0])
        done(left(kh, pl.ds(0, 3 * SIDE)), sem_s.at[1])
        for group in range(2, 6):
            done(left(vh, pl.ds(0, 6)), sem_s.at[group])
        done(st_recv.at[0 : SIDE - 1], sem_s.at[6])
        if rows_n > 1:
            done(ssq_recv.at[1:rows_n], sem_s.at[7])
        done(st_recv.at[0 : SIDE - 1], sem_s.at[8])


def on_device(rows_n, queries, keys, values, gain_q, gain_k, clip_ids, clip_grid):
    T, width = queries.shape
    freq, cut_a, cut_b = frequencies()
    bf, f32 = jnp.bfloat16, jnp.float32
    vm = pl.BlockSpec(memory_space=pltpu.VMEM)
    dma = pltpu.SemaphoreType.DMA
    block = (T, HD)
    return pl.pallas_call(
        functools.partial(kernel, rows_n, float(width * rows_n), cut_a, cut_b),
        out_shape=pltpu.VMEM((T, width), bf),
        in_specs=[pl.BlockSpec(memory_space=pltpu.HBM)] * 8,
        out_specs=vm,
        scratch_shapes=[
            pltpu.VMEM((T, width), bf),
            pltpu.VMEM((T, width), bf),
            pltpu.VMEM((width,), f32),
            pltpu.VMEM((width,), f32),
            pltpu.VMEM((1, T), jnp.int32),
            pltpu.VMEM((1, HD), f32),
            pltpu.VMEM((2, CLIPS), jnp.int32),
            pltpu.VMEM((SIDE * T + 64, HD), f32),
            pltpu.VMEM((8, 256), f32),
            pltpu.VMEM((rows_n, 8, 256), f32),
            pltpu.VMEM((8, HD), f32),
            pltpu.VMEM((SIDE, 8, HD), f32),
            pltpu.VMEM((8, HD), f32),
            pltpu.VMEM((SIDE, 8, HD), f32),
            pltpu.VMEM((T, width), bf),
            pltpu.VMEM((T, width), bf),
            pltpu.VMEM((SIDE * SIDE, T, 2 * HD), bf),
            pltpu.VMEM((SIDE * SIDE, T, 2 * HD), bf),
            pltpu.VMEM((SIDE, T, 2 * HD), bf),
            pltpu.VMEM((SIDE, T, 2 * HD), bf),
            pltpu.VMEM((SIDE, T, 2 * HD), bf),
            pltpu.VMEM((SIDE, T, 2 * HD), bf),
            pltpu.VMEM((SIDE * T, HD), f32),
            pltpu.VMEM((3, SIDE * T // 3, 2 * SIDE * T), f32),
            pltpu.VMEM((SIDE * T, 2 * HD), f32),
            pltpu.VMEM((SIDE,) + block, bf),
            pltpu.VMEM((SIDE,) + block, bf),
            pltpu.VMEM((SIDE,) + block, bf),
            pltpu.VMEM((SIDE, 8, 256), f32),
            pltpu.VMEM((SIDE, 8, 256), f32),
            pltpu.VMEM((8, HD), f32),
            dma((9,)),
            dma((9,)),
            dma((3, SIDE)),
            dma((2, 2)),
            dma((9,)),
        ],
        compiler_params=pltpu.CompilerParams(
            collective_id=0, has_side_effects=True, vmem_limit_bytes=48 * 1024 * 1024
        ),
        name="clip_attention",
    )(*[pltpu.with_memory_space_constraint(a, pltpu.HBM) for a in (
        queries, keys, values, gain_q, gain_k, clip_ids[None, :], jnp.asarray(freq), clip_grid.T,
    )])


def solution(mesh):
    in_specs = (
        P(("batch", "ctx"), "row"),
        P(("batch", "ctx"), "row"),
        P(("batch", "ctx"), "row"),
        P("row"),
        P("row"),
        P(("batch", "ctx")),
        P("batch", None),
    )
    out_specs = P(("batch", "ctx"), "row")
    return jax.shard_map(
        functools.partial(on_device, mesh.shape["row"]),
        mesh=mesh, in_specs=in_specs, out_specs=out_specs, check_vma=False,
    )
```

```python
import functools
import math

import jax
import jax.numpy as jnp
import numpy as np
from jax import lax
from jax.experimental import pallas as pl
from jax.experimental.pallas import tpu as pltpu
from jax.sharding import PartitionSpec as P

HD = 128
CLIPS = 4
EPSILON = 1e-06
NEGATIVE = -1e30
ROTARY_BASE = 10000.0
LOG2E = math.log2(math.e)
SIDE = 4
MESH = pl.DeviceIdType.MESH


def frequencies():
    p = HD // 6
    f = HD - 4 * p
    base = np.float32(ROTARY_BASE)
    first = np.float32(1.0) / base ** (np.arange(0, f, 2, dtype=np.float32) / np.float32(f))
    other = np.float32(1.0) / base ** (np.arange(0, 2 * p, 2, dtype=np.float32) / np.float32(2 * p))
    return np.repeat(np.concatenate([first, other, other]), 2)[None, :].astype(np.float32), f, f + 2 * p


def cols(h):
    if isinstance(h, int):
        return pl.ds(h * HD, HD)
    return pl.ds(pl.multiple_of(h * HD, HD), HD)


def kernel(
    rows_n, model, cut_a, cut_b,
    q_hbm, k_hbm, v, gq_hbm, gk_hbm, ids_hbm, freq_hbm, grid_hbm, out,
    q, k, gq, gk, ids, freq, grid, pad, ssq_send, ssq_recv, cz_send, cz_recv, cx_send, cx_recv,
    krot, qrot, kh, vh, k4, v4, qh, q4, m_scr, s_scr, a_scr, o_send, o4_send, o4_recv, st_send, st_recv, starts_scr,
    sem_s, sem_r, sem_zr, sem_xr, sem_in,
):
    T = q.shape[0]
    me = lax.axis_index("ctx")
    row = lax.axis_index("row")
    x = me // SIDE
    z = lax.rem(me, SIDE)
    zs = [lax.rem(z + d, SIDE) for d in range(SIDE)]
    xs = [lax.rem(x + d, SIDE) for d in range(SIDE)]
    zpeer = [x * SIDE + a for a in zs]
    xpeer = [a * SIDE + z for a in xs]
    zsrc = [lax.rem(z + SIDE - d, SIDE) for d in range(SIDE)]
    xsrc = [lax.rem(x + SIDE - d, SIDE) for d in range(SIDE)]
    scale = 1.0 / math.sqrt(HD)
    wide = SIDE * T

    def left(ref, i):
        return ref.at[i, :, 0:HD]

    loads = [
        pltpu.make_async_copy(src, dst, sem_in.at[i])
        for i, (src, dst) in enumerate([
            (ids_hbm, ids), (q_hbm, q), (k_hbm, k), (grid_hbm, grid), (freq_hbm, freq),
            (gk_hbm, gk), (gq_hbm, gq), (v.at[:, cols(z)], left(vh, z)), (v.at[:, cols(4)], left(v4, z)),
        ])
    ]
    loads[0].start()
    barrier = pltpu.get_barrier_semaphore()
    for d in range(1, SIDE):
        pl.semaphore_signal(barrier, inc=1, device_id={"ctx": zpeer[d]}, device_id_type=MESH)
        pl.semaphore_signal(barrier, inc=1, device_id={"ctx": xpeer[d]}, device_id_type=MESH)
    for d in range(1, rows_n):
        pl.semaphore_signal(
            barrier, inc=1, device_id={"row": lax.rem(row + d, rows_n)}, device_id_type=MESH
        )
    for c in loads[1:]:
        c.start()

    def send(src, dst, group, arrival, where):
        pltpu.make_async_remote_copy(
            src_ref=src, dst_ref=dst, send_sem=sem_s.at[group], recv_sem=arrival, device_id=where,
            device_id_type=MESH,
        ).start()

    def done(ref, sem):
        pltpu.make_async_copy(ref, ref, sem).wait()

    def to_z(n, src, dst):
        for d in (1, 3, 2):
            send(src.at[:, cols(zs[d])], dst, 2 + n, sem_zr.at[n, d], {"ctx": zpeer[d]})

    def four_to_z(n, src, dst):
        for d in (2, 1, 3) if n else (1, 3, 2):
            send(src.at[:, cols(4)], left(dst, z), 2 + n, sem_r.at[n], {"ctx": zpeer[d]})

    def to_near(n, src, dst, a):
        for g, d in ((1, 1), (2, 3)):
            send(src, left(dst, g * SIDE + a), n, sem_xr.at[n, 0], {"ctx": xpeer[d]})

    def to_far(n, src, dst, a):
        send(src, left(dst, 3 * SIDE + a), n, sem_xr.at[n, 1], {"ctx": xpeer[2]})

    loads[0].wait()
    level = lax.broadcasted_iota(jnp.int32, (8, T), 0)
    below = jnp.where(jnp.broadcast_to(ids[...], (8, T)) < level, 1.0, 0.0).astype(jnp.float32)
    cz_send[...] = jnp.broadcast_to(jnp.sum(below, axis=1, keepdims=True), (8, HD))

    with jax.named_scope("entry_wait"):
        pl.semaphore_wait(barrier, 2 * (SIDE - 1) + rows_n - 1)

    for d in range(1, SIDE):
        send(cz_send, cz_recv.at[d], 6, sem_r.at[3], {"ctx": zpeer[d]})
    to_z(0, v, left(vh, z))
    to_near(0, v.at[:, cols(z)], vh, z)
    to_far(0, v.at[:, cols(z)], vh, z)

    with jax.named_scope("squares"):
        pad[T:256, :] = jnp.zeros((256 - T, HD), jnp.float32)
        ssq_send[...] = jnp.zeros_like(ssq_send)
        for i, ref in enumerate((q, k)):
            loads[1 + i].wait()
            acc = None
            for h in range(5):
                w = ref[:, h * HD : (h + 1) * HD].astype(jnp.float32)
                acc = w * w if acc is None else acc + w * w
            pad[:T, :] = acc
            ssq_send[i : i + 1, :] = jnp.sum(jnp.transpose(pad[0:256, :]), axis=0, keepdims=True)
    for d in range(1, rows_n):
        send(
            ssq_send, ssq_recv.at[d], 7, sem_r.at[5], {"row": lax.rem(row + d, rows_n)}
        )

    with jax.named_scope("count_z_wait"):
        done(cz_recv.at[1:SIDE], sem_r.at[3])
    part = cz_send[...]
    for d in range(1, SIDE):
        part = part + cz_recv[d]
    cx_send[...] = part
    for d in range(1, SIDE):
        send(cx_send, cx_recv.at[d], 6, sem_r.at[4], {"ctx": xpeer[d]})

    def forward(n, ref, j):
        slot = left(ref, zsrc[j])
        with jax.named_scope("%s_wait%d" % ("vk"[n], j)):
            done(slot, sem_zr.at[n, j])
        to_near(n, slot, ref, zsrc[j])
        if n == 0:
            to_far(n, slot, ref, zsrc[j])

    four_to_z(0, v, v4)
    forward(0, vh, 1)
    forward(0, vh, 3)
    with jax.named_scope("count_x_wait"):
        done(cx_recv.at[1:SIDE], sem_r.at[4])
    starts = cx_send[...]
    for d in range(1, SIDE):
        starts = starts + cx_recv[d]
    starts_scr[...] = starts

    for c in loads[3:]:
        c.wait()
    lane = lax.broadcasted_iota(jnp.int32, (T, HD), 1)
    token = (lax.broadcasted_iota(jnp.int32, (T, HD), 0) + me * T).astype(jnp.float32)
    first = jnp.zeros((T, HD), jnp.float32)
    shape_of = grid[...].astype(jnp.float32)
    height = jnp.broadcast_to(shape_of[0:1, 0:1], (T, HD))
    width = jnp.broadcast_to(shape_of[1:2, 0:1], (T, HD))
    for c in range(1, CLIPS):
        s = jnp.broadcast_to(starts[c : c + 1, :], (T, HD))
        inside = token >= s
        first = jnp.where(inside, s, first)
        height = jnp.where(inside, shape_of[0:1, c : c + 1], height)
        width = jnp.where(inside, shape_of[1:2, c : c + 1], width)
    offset = token - first
    frame = jnp.floor((offset + 0.5) / (height * width))
    lines = jnp.floor((offset + 0.5) / width)
    line = lines - height * jnp.floor((lines + 0.5) / height)
    column = offset - width * lines
    place = jnp.where(lane < cut_a, frame, jnp.where(lane < cut_b, line, column))
    angle = place * freq[...]
    with jax.named_scope("trig"):
        cosine = jnp.cos(angle)
    even = lax.rem(lane, 2) == 0
    sine = jnp.sin(angle)

    with jax.named_scope("square_wait"):
        if rows_n > 1:
            done(ssq_recv.at[1:rows_n], sem_r.at[5])
    total = ssq_send[...]
    for d in range(1, rows_n):
        total = total + ssq_recv[d]
    rs = lax.rsqrt(total / model + EPSILON)

    def rope(src, dst, gain, i):
        col = jnp.transpose(jnp.broadcast_to(rs[i : i + 1, :], (HD, rs.shape[1])))[:T, :]
        for h in (4, 0, 1, 2, 3):
            a = src[:, h * HD : (h + 1) * HD].astype(jnp.float32) * col
            a = a * gain[h * HD : (h + 1) * HD].reshape(1, HD)
            partner = jnp.where(even, -pltpu.roll(a, HD - 1, 1), pltpu.roll(a, 1, 1))
            dst[:, h * HD : (h + 1) * HD] = (a * cosine + partner * sine).astype(jnp.bfloat16)

    with jax.named_scope("rope_k"):
        rope(k, krot, gk, 1)
    to_z(1, krot, left(kh, z))
    to_near(1, krot.at[:, cols(z)], kh, z)
    to_far(1, krot.at[:, cols(z)], kh, z)
    forward(0, vh, 2)
    with jax.named_scope("rope_q"):
        rope(q, qrot, gq, 0)
    for d in (1, 3, 2):
        send(qrot.at[:, cols(zs[d])], left(qh, z), 4, sem_zr.at[2, d], {"ctx": zpeer[d]})
    kh[z, :, 0:HD] = krot[:, cols(z)]
    k4[z, :, 0:HD] = krot[:, cols(4)]
    qh[z, :, 0:HD] = qrot[:, cols(z)]
    q4[x, :, 0:HD] = qrot[:, cols(4)]

    lanes = lax.broadcasted_iota(jnp.int32, (T, HD), 1)

    def member(first_token, inside, outside):
        t = (lax.broadcasted_iota(jnp.int32, (T, HD), 0) + first_token).astype(jnp.float32)
        c = jnp.zeros((T, HD), jnp.int32)
        for i in range(1, CLIPS):
            c = c + jnp.where(t >= starts_scr[i : i + 1, :], 1, 0)
        value = jnp.where(c == lanes, inside, outside)
        return jnp.where(lanes < CLIPS, value, 0.0).astype(jnp.bfloat16)

    ones = jnp.ones((T, HD), jnp.bfloat16)

    def fill(g, d):
        def body(i, carry):
            vh[g * SIDE + i, :, HD:] = ones
            kh[g * SIDE + i, :, HD:] = member((xsrc[d] * SIDE + i) * T, 1.0, 0.0)
            return carry

        lax.fori_loop(0, SIDE, body, 0)

    def fill_four(i, carry):
        v4[i, :, HD:] = ones
        k4[i, :, HD:] = member((x * SIDE + i) * T, 1.0, 0.0)
        qh[i, :, HD:] = member((x * SIDE + i) * T, 0.0, NEGATIVE)
        q4[i, :, HD:] = member((i * SIDE + z) * T, 0.0, NEGATIVE)
        return carry

    with jax.named_scope("fill"):
        lax.fori_loop(0, SIDE, fill_four, 0)
        for g, d in enumerate((0, 1, 3, 2)):
            fill(g, d)
    for j in (1, 3, 2):
        forward(1, kh, j)
    for j in (1, 3, 2):
        to_far(1, left(kh, zsrc[j]), kh, zsrc[j])
    for d in (1, 3, 2):
        send(qrot.at[:, cols(4)], left(q4, x), 4, sem_r.at[2], {"ctx": xpeer[d]})

    third = wide // 3

    def attend(queries, keys, vals, carried=None):
        keys = keys.reshape(-1, 2 * HD)
        vals = vals.reshape(-1, 2 * HD)
        n = keys.shape[0]
        for t in range(3):
            tile = pl.ds(t * third, third)
            s = lax.dot_general(
                queries[t * third : (t + 1) * third], keys, (((1,), (1,)), ((), ())),
                preferred_element_type=jnp.float32,
            )
            s_scr[t, :, 0:n] = s
            m = jnp.max(s, axis=1, keepdims=True)
            if carried:
                old = m_scr[tile, 0:1]
                m = jnp.maximum(m, old)
                factor = jnp.exp2((old - m) * (scale * LOG2E))
            w = jnp.exp2((s_scr[t, :, 0:n] - m) * (scale * LOG2E)).astype(jnp.bfloat16)
            o = jnp.dot(w, vals, preferred_element_type=jnp.float32)
            if carried:
                o = o + a_scr[tile, :] * factor
            a_scr[tile, :] = o
            m_scr[tile, :] = jnp.broadcast_to(m, (third, HD))

    def divide(o):
        return (o[:, :HD] / o[:, HD:]).astype(jnp.bfloat16)

    with jax.named_scope("q_wait"):
        for n in (3, 1, 2):
            done(left(qh, zs[n]), sem_zr.at[2, SIDE - n])
    four_to_z(1, krot, k4)
    with jax.named_scope("own_attend"):
        attend(qh[...].reshape(wide, 2 * HD), kh[0:SIDE], vh[0:SIDE])
    queries = qh[...].reshape(wide, 2 * HD)
    for name, side, first, last in (("near", 0, SIDE, 3 * SIDE), ("far", 1, 3 * SIDE, 4 * SIDE)):
        with jax.named_scope(name + "_wait"):
            done(left(vh, pl.ds(first, last - first)), sem_xr.at[0, side])
            done(left(kh, pl.ds(first, last - first)), sem_xr.at[1, side])
        with jax.named_scope(name + "_attend"):
            attend(queries, kh[first:last], vh[first:last], True)
    with jax.named_scope("divide"):
        o_send[...] = divide(a_scr[...]).reshape(SIDE, T, HD)
    for n in (2, 1, 3):
        send(o_send.at[zs[n]], out.at[:, cols(z)], 5, sem_r.at[6], {"ctx": zpeer[n]})
    out[:, cols(z)] = o_send[z]

    with jax.named_scope("four_wait"):
        done(left(v4, pl.ds(0, SIDE - 1)), sem_r.at[0])
        done(left(k4, pl.ds(0, SIDE - 1)), sem_r.at[1])
        done(left(q4, pl.ds(0, SIDE - 1)), sem_r.at[2])
    with jax.named_scope("four_attend"):
        pad[wide:, :] = jnp.zeros((64, HD), jnp.float32)
        attend(q4[...].reshape(wide, 2 * HD), k4[...], v4[...])
        o4_send[...] = divide(a_scr[...]).reshape(SIDE, T, HD)
    for d in (2, 1, 3):
        send(o4_send.at[xs[d]], o4_recv.at[x], 5, sem_r.at[7], {"ctx": xpeer[d]})
    with jax.named_scope("stats"):
        flags = lax.broadcasted_iota(jnp.int32, (wide, HD), 1)
        pad[0:wide, :] = jnp.where(
            flags == 0, m_scr[...] * scale, jnp.where(flags == 1, a_scr[:, HD:], 0.0)
        )
        for i in range(SIDE):
            st_send[i] = jnp.transpose(pad[i * T : i * T + 256, :])[:8, :]
    for d in (2, 1, 3):
        send(st_send.at[xs[d]], st_recv.at[x], 8, sem_r.at[8], {"ctx": xpeer[d]})
    o4_recv[x] = o4_send[x]
    st_recv[x] = st_send[x]
    with jax.named_scope("four_back_wait"):
        done(o4_recv.at[0 : SIDE - 1], sem_r.at[7])
        done(st_recv.at[0 : SIDE - 1], sem_r.at[8])
    peaks = [st_recv[i, 0:1, :] for i in range(SIDE)]
    peak = functools.reduce(jnp.maximum, peaks)
    shares = [st_recv[i, 1:2, :] * jnp.exp(peaks[i] - peak) for i in range(SIDE)]
    whole = functools.reduce(jnp.add, shares)
    line = lax.broadcasted_iota(jnp.int32, (HD, st_recv.shape[2]), 0)
    table = jnp.zeros((HD, st_recv.shape[2]), jnp.float32)
    for i in range(SIDE):
        table = jnp.where(line == i, shares[i] / whole, table)
    share = jnp.transpose(table)[:T, :]
    num = jnp.zeros((T, HD), jnp.float32)
    for i in range(SIDE):
        num = num + share[:, i : i + 1] * o4_recv[i].astype(jnp.float32)
    out[:, cols(4)] = num.astype(jnp.bfloat16)

    with jax.named_scope("back_wait"):
        done(o4_recv.at[0 : SIDE - 1], sem_r.at[6])
    with jax.named_scope("send_wait"):
        done(left(vh, pl.ds(0, 3 * SIDE)), sem_s.at[0])
        done(left(kh, pl.ds(0, 3 * SIDE)), sem_s.at[1])
        for group in range(2, 6):
            done(left(vh, pl.ds(0, 6)), sem_s.at[group])
        done(st_recv.at[0 : SIDE - 1], sem_s.at[6])
        if rows_n > 1:
            done(ssq_recv.at[1:rows_n], sem_s.at[7])
        done(st_recv.at[0 : SIDE - 1], sem_s.at[8])


def on_device(rows_n, queries, keys, values, gain_q, gain_k, clip_ids, clip_grid):
    T, width = queries.shape
    freq, cut_a, cut_b = frequencies()
    bf, f32 = jnp.bfloat16, jnp.float32
    vm = pl.BlockSpec(memory_space=pltpu.VMEM)
    dma = pltpu.SemaphoreType.DMA
    block = (T, HD)
    return pl.pallas_call(
        functools.partial(kernel, rows_n, float(width * rows_n), cut_a, cut_b),
        out_shape=pltpu.VMEM((T, width), bf),
        in_specs=[pl.BlockSpec(memory_space=pltpu.HBM)] * 8,
        out_specs=vm,
        scratch_shapes=[
            pltpu.VMEM((T, width), bf),
            pltpu.VMEM((T, width), bf),
            pltpu.VMEM((width,), f32),
            pltpu.VMEM((width,), f32),
            pltpu.VMEM((1, T), jnp.int32),
            pltpu.VMEM((1, HD), f32),
            pltpu.VMEM((2, CLIPS), jnp.int32),
            pltpu.VMEM((SIDE * T + 64, HD), f32),
            pltpu.VMEM((8, 256), f32),
            pltpu.VMEM((rows_n, 8, 256), f32),
            pltpu.VMEM((8, HD), f32),
            pltpu.VMEM((SIDE, 8, HD), f32),
            pltpu.VMEM((8, HD), f32),
            pltpu.VMEM((SIDE, 8, HD), f32),
            pltpu.VMEM((T, width), bf),
            pltpu.VMEM((T, width), bf),
            pltpu.VMEM((SIDE * SIDE, T, 2 * HD), bf),
            pltpu.VMEM((SIDE * SIDE, T, 2 * HD), bf),
            pltpu.VMEM((SIDE, T, 2 * HD), bf),
            pltpu.VMEM((SIDE, T, 2 * HD), bf),
            pltpu.VMEM((SIDE, T, 2 * HD), bf),
            pltpu.VMEM((SIDE, T, 2 * HD), bf),
            pltpu.VMEM((SIDE * T, HD), f32),
            pltpu.VMEM((3, SIDE * T // 3, 2 * SIDE * T), f32),
            pltpu.VMEM((SIDE * T, 2 * HD), f32),
            pltpu.VMEM((SIDE,) + block, bf),
            pltpu.VMEM((SIDE,) + block, bf),
            pltpu.VMEM((SIDE,) + block, bf),
            pltpu.VMEM((SIDE, 8, 256), f32),
            pltpu.VMEM((SIDE, 8, 256), f32),
            pltpu.VMEM((8, HD), f32),
            dma((9,)),
            dma((9,)),
            dma((3, SIDE)),
            dma((2, 2)),
            dma((9,)),
        ],
        compiler_params=pltpu.CompilerParams(
            collective_id=0, has_side_effects=True, vmem_limit_bytes=48 * 1024 * 1024
        ),
        name="clip_attention",
    )(*[pltpu.with_memory_space_constraint(a, pltpu.HBM) for a in (
        queries, keys, values, gain_q, gain_k, clip_ids[None, :], jnp.asarray(freq), clip_grid.T,
    )])


def solution(mesh):
    in_specs = (
        P(("batch", "ctx"), "row"),
        P(("batch", "ctx"), "row"),
        P(("batch", "ctx"), "row"),
        P("row"),
        P("row"),
        P(("batch", "ctx")),
        P("batch", None),
    )
    out_specs = P(("batch", "ctx"), "row")
    return jax.shard_map(
        functools.partial(on_device, mesh.shape["row"]),
        mesh=mesh, in_specs=in_specs, out_specs=out_specs, check_vma=False,
    )
```
